128 devices in a mesh: dp: 4 (over y), tm: 4 (over x), rows: 8 (over z, core).
Axes of the slice: x: 4, y: 4, z: 4, core: 2. Of those that a mesh axis runs over, the one named last changes fastest.
Arguments:
- latents: bfloat16 [4, 8, 32, 32, 384], P('dp', 'tm', 'rows'), may hold values from -6 to 6
- hidden: bfloat16 [4, 8, 32, 32, 384], P('dp', 'tm', 'rows'), may hold values from -8 to 8
- cotangent: bfloat16 [4, 8, 32, 32, 384], P('dp', 'tm', 'rows'), may hold values from -6 to 6
- conv_one: bfloat16 [3, 3, 3, 384, 384], replicated, may hold values from -0.0625 to 0.0625
- conv_two: bfloat16 [3, 3, 3, 384, 384], replicated, may hold values from -0.0625 to 0.0625
- lengths: int32 [4], P('dp'), may hold values from 3 to 8, as said below
Outputs:
- latent_grad: float32 [4, 8, 32, 32, 384], P('dp', None, None, ('tm', 'rows'))
The draws below stay inside these ranges and needn't reach their ends.
Inputs may be any that keep to these rules, and one draw needn't show every extreme that they name: `lengths`: at least one clip has all 8 frames valid.
All inputs are finite; a program needn't handle non-finite values.
Results may differ from the reference program's by a relative error of at most 0.00092.
Values may be sent and summed in bfloat16 or wider, within the bound.
A program may use at most 64 MiB of HBM per device.

```python
import jax
import jax.numpy as jnp
from jax import lax

C = 384
FRAME_DEV = 2
COLS = 32
FRAMES = 8
ROWS_ALL = 32
CLIPS = 4


def draw_lengths(key, part):
    drawn_counts = jax.random.randint(jax.random.fold_in(key, 11), (CLIPS,), FRAME_DEV + 1, FRAMES + 1)
    full_clip = jax.random.randint(jax.random.fold_in(key, 12), (), 0, CLIPS)
    return jnp.where(jnp.arange(CLIPS) == full_clip, FRAMES, drawn_counts).astype(jnp.int32)


def block_scale(key, extent, pieces, least, high):
    gain = 1.0
    for axis_at, blocks in pieces:
        heights = jax.random.uniform(jax.random.fold_in(jax.random.fold_in(key, 6), axis_at), (blocks,), jnp.float32, least / len(pieces), high / len(pieces))
        gain = gain * jnp.repeat(jnp.exp(heights), extent[axis_at] // blocks).reshape((-1,) + (1,) * (len(extent) - 1 - axis_at))
    return gain


def scatter_about(own_key, extent, deviation, bound, cuts=(), held_as=jnp.bfloat16):
    entries = jax.random.normal(own_key, extent, jnp.float32) * deviation
    if len(cuts) > 0:
        entries = block_scale(own_key, extent, cuts, -0.22, 0.18) * entries
    return jnp.clip(entries, min=-bound, max=bound).astype(held_as)


def setup_inputs(seed: int = 0) -> dict:
    key_list = jax.random.split(jax.random.key(seed), 7)
    return {
        "latents": scatter_about(key_list[0], (CLIPS, FRAMES, ROWS_ALL, COLS, C), 1.0, 6.0, ((0, 4), (1, 4), (2, 8))),
        "hidden": scatter_about(key_list[1], (CLIPS, FRAMES, ROWS_ALL, COLS, C), 2.0, 8.0, ((0, 4), (1, 4), (2, 8))),
        "cotangent": scatter_about(key_list[2], (CLIPS, FRAMES, ROWS_ALL, COLS, C), 1.0, 6.0, ((0, 4), (1, 4), (2, 8))),
        "conv_one": scatter_about(key_list[3], (3, 3, 3, C, C), (27 * C) ** -0.5, 0.0625),
        "conv_two": scatter_about(key_list[4], (3, 3, 3, C, C), (27 * C) ** -0.5, 0.0625),
        "lengths": draw_lengths(jax.random.fold_in(key_list[6], 71), 0),
    }


def silu_slope(values):
    sigmoid_of = jax.nn.sigmoid(values)
    return sigmoid_of * (1.0 + values * (1.0 - sigmoid_of))


def transposed(padded, kernel):
    flipped = jnp.flip(kernel, (0, 1, 2)).transpose(0, 1, 2, 4, 3)
    return lax.conv_general_dilated(padded, flipped, (1, 1, 1), "VALID", dimension_numbers=("NDHWC", "DHWIO", "NDHWC"), preferred_element_type=jnp.float32)


def reference(latents, hidden, cotangent, conv_one, conv_two, lengths):
    frames = jnp.arange(FRAMES, dtype=jnp.int32)
    live_frames = frames[None, :] < lengths[:, None]
    masked = jnp.where(live_frames[:, :, None, None, None], cotangent, jnp.zeros_like(cotangent))
    pad_spec = ((0, 0), (0, 2), (1, 1), (1, 1), (0, 0))
    grad_act = transposed(jnp.pad(masked, pad_spec), conv_two)
    grad_hidden = (grad_act * silu_slope(hidden.astype(jnp.float32))).astype(jnp.bfloat16)
    grad_input = transposed(jnp.pad(grad_hidden, pad_spec), conv_one)
    return masked.astype(jnp.float32) + grad_input * silu_slope(latents.astype(jnp.float32))
```

```python
import functools

import jax
import jax.numpy as jnp
from jax import lax
from jax.experimental import pallas as pl
from jax.experimental.pallas import tpu as pltpu
from jax.sharding import PartitionSpec as P

MESH = pl.DeviceIdType.MESH
NT = (((1,), (1,)), ((), ()))
F32 = jnp.float32
BF16 = jnp.bfloat16
SPLIT = 256


def silu_slope(values):
    gate = 1.0 / (1.0 + jnp.exp(-values))
    return gate * (1.0 + values * (1.0 - gate))


def kernel(
    sizes,
    len_ref,
    cot_ref,
    hid_ref,
    lat_ref,
    w_two,
    w_one,
    out_ref,
    wv_two,
    wv_one,
    tmp,
    tmp_back,
    stage_c,
    stage_h,
    recv_c,
    recv_h,
    cots,
    grads,
    acc,
    slope_h,
    slope_l,
    w_sem,
    c_send,
    c_recv,
    h_send,
    h_recv,
    x_send,
    x_recv,
    ga_send,
    ga_recv,
    gb_send,
    gb_recv,
):
    tms, rws, fd, rd, cols, ch = sizes
    group = tms * rws
    frames = tms * fd
    rows = rws * rd
    pix = frames * rows
    dp = lax.axis_index("dp")
    tm = lax.axis_index("tm")
    rw = lax.axis_index("rows")
    me = tm * rws + rw

    def peer(k):
        d_tm = lax.rem(tm + k // rws, tms)
        d_rw = lax.rem(rw + lax.rem(k, rws), rws)
        return d_tm, d_rw

    barrier = pltpu.get_barrier_semaphore()

    def greet(k, carry):
        d_tm, d_rw = peer(k)
        pl.semaphore_signal(barrier, inc=1, device_id=(dp, d_tm, d_rw), device_id_type=MESH)
        return carry

    lax.fori_loop(1, group, greet, 0)

    weight_copies = []
    for n, (src, dst) in enumerate(((w_two, wv_two), (w_one, wv_one))):
        for at, c in enumerate((1, 0, 2)):
            copy = pltpu.make_async_copy(src.at[:, :, c], dst.at[:, :, c], w_sem.at[n, at])
            copy.start()
            weight_copies.append(copy)

    lanes = out_ref.shape[1]
    strips = ch // lanes
    row_of = lax.broadcasted_iota(jnp.int32, (fd * rd, lanes), 0)
    live = tm * fd + row_of // rd < len_ref[0]

    def columns_of(src_ref, dst_ref, at, masked):
        for j in range(strips):
            tmp[j] = src_ref[:, j * lanes : (j + 1) * lanes].astype(F32)

        def one(w, carry):
            for j in range(strips):
                block = tmp.at[j][pl.ds(w, fd * rd, stride=cols), :]
                if masked:
                    block = jnp.where(live, block, 0.0)
                dst_ref[w, at : at + fd * rd, j * lanes : (j + 1) * lanes] = block.astype(BF16)
            return carry

        lax.fori_loop(0, cols, one, 0)

    def send_all(stage, recv, send_sem, recv_sem):
        def one(k, carry):
            d_tm, d_rw = peer(k)
            pltpu.make_async_remote_copy(
                src_ref=stage.at[d_tm * rws + d_rw],
                dst_ref=recv.at[me],
                send_sem=send_sem,
                recv_sem=recv_sem,
                device_id=(dp, d_tm, d_rw),
                device_id_type=MESH,
            ).start()
            return carry

        lax.fori_loop(1, group, one, 0)

    def wait_all(recv, sem):
        part = recv.at[pl.ds(0, group - 1)]
        pltpu.make_async_copy(part, part, sem).wait()

    columns_of(cot_ref, stage_c, 0, True)
    pl.semaphore_wait(barrier, group - 1)
    send_all(stage_c, recv_c, c_send, c_recv)
    columns_of(hid_ref, stage_h, 0, False)
    columns_of(lat_ref, stage_h, fd * rd, False)
    send_all(stage_h, recv_h, h_send, h_recv)
    recv_c[pl.ds(me, 1)] = stage_c[pl.ds(me, 1)]
    recv_h[pl.ds(me, 1)] = stage_h[pl.ds(me, 1)]

    tail = cots.shape[1] - pix
    for buf in (cots, grads):
        buf[:, pl.ds(pix, tail), :] = jnp.zeros((3, tail, ch), BF16)

        @pl.when(me == 0)
        def _():
            buf[2, pl.ds(0, pix), :] = jnp.zeros((pix, ch), BF16)

        @pl.when(me == group - 1)
        def _():
            buf[0, pl.ds(0, pix), :] = jnp.zeros((pix, ch), BF16)

    def gather_rows(recv, at):
        for t in range(tms):
            for pair in range(rws // 2):
                one = recv[t * rws + 2 * pair, at : at + fd * rd, :].astype(F32)
                two = recv[t * rws + 2 * pair + 1, at : at + fd * rd, :].astype(F32)
                for f in range(fd):
                    joined = jnp.concatenate([one[f * rd : (f + 1) * rd], two[f * rd : (f + 1) * rd]], axis=0)
                    start = (t * fd + f) * rows + 2 * pair * rd
                    tmp_back[start : start + 2 * rd, :] = joined

    def to_neighbours(buf, chans, send_sem, recv_sem):
        copies = []
        for to, has, slot in ((me + 1, me < group - 1, 2), (me - 1, me > 0, 0)):
            to = lax.rem(to + group, group)
            copies.append((
                has,
                pltpu.make_async_remote_copy(
                    src_ref=buf.at[1, pl.ds(0, pix), chans],
                    dst_ref=buf.at[slot, pl.ds(0, pix), chans],
                    send_sem=send_sem.at[slot],
                    recv_sem=recv_sem.at[slot],
                    device_id=(dp, to // rws, lax.rem(to, rws)),
                    device_id_type=MESH,
                ),
            ))
        for has, copy in copies:
            pl.when(has)(copy.start)
        return copies

    def wait_recv(copies):
        pl.when(me > 0)(copies[0][1].wait_recv)
        pl.when(me < group - 1)(copies[1][1].wait_recv)

    def wait_send(copies):
        for has, copy in copies:
            pl.when(has)(copy.wait_send)

    wait_all(recv_c, c_recv)
    gather_rows(recv_c, 0)
    cots[1, pl.ds(0, pix), :] = tmp_back[...].astype(BF16)
    x_copies = to_neighbours(cots, pl.ds(0, ch), x_send, x_recv)

    def stacked(buf, columns, ins):
        parts = [buf[c, (2 - a) * rows : (2 - a) * rows + pix, ins] for c in columns for a in range(3)]
        return jnp.concatenate(parts, axis=1)

    def weights(wv, columns, outs, ins):
        return jnp.concatenate(
            [
                jnp.concatenate([wv[a, r, c, outs, ins] for c in columns for a in range(3)], axis=1)
                for r in range(3)
            ],
            axis=0,
        )

    def product(buf, wv, columns, outs, ins):
        return lax.dot_general(
            stacked(buf, columns, ins), weights(wv, columns, outs, ins), NT, preferred_element_type=F32
        )

    every = slice(0, ch)

    def row_taps(above, same, below):
        at_row = lax.rem(lax.broadcasted_iota(jnp.int32, above.shape, 0), rows)
        up = jnp.where(at_row == rows - 1, 0.0, pltpu.roll(above, pix - 1, 0))
        down = jnp.where(at_row == 0, 0.0, pltpu.roll(below, 1, 0))
        return same + up + down

    weight_copies[0].wait()
    acc[...] = product(cots, wv_two, (1,), every, every)

    wait_all(recv_h, h_recv)
    gather_rows(recv_h, 0)
    slope_h[...] = silu_slope(tmp_back[...])
    gather_rows(recv_h, fd * rd)
    slope_l[...] = silu_slope(tmp_back[...])

    weight_copies[1].wait()
    weight_copies[2].wait()
    wait_recv(x_copies)
    g_copies = []
    for outs, send_sem, recv_sem in ((slice(0, SPLIT), ga_send, ga_recv), (slice(SPLIT, ch), gb_send, gb_recv)):
        part = product(cots, wv_two, (0, 2), outs, every)
        n = outs.stop - outs.start
        taps = [
            acc[:, r * ch + outs.start : r * ch + outs.stop] + part[:, r * n : (r + 1) * n] for r in range(3)
        ]
        grads[1, pl.ds(0, pix), outs] = (row_taps(*taps) * slope_h[:, outs]).astype(BF16)
        g_copies.append(to_neighbours(grads, pl.ds(outs.start, n), send_sem, recv_sem))

    weight_copies[3].wait()
    acc[...] = product(grads, wv_one, (1,), every, every)
    weight_copies[4].wait()
    weight_copies[5].wait()
    wait_recv(g_copies[0])
    acc[...] += product(grads, wv_one, (0, 2), every, slice(0, SPLIT))
    wait_recv(g_copies[1])
    part = product(grads, wv_one, (0, 2), every, slice(SPLIT, ch))
    taps = [acc[:, r * ch : (r + 1) * ch] + part[:, r * ch : (r + 1) * ch] for r in range(3)]
    result = cots[1, pl.ds(0, pix), :].astype(F32) + row_taps(*taps) * slope_l[...]
    for j in range(strips):
        out_ref[pl.ds(j, pix, stride=strips), :] = result[:, j * lanes : (j + 1) * lanes]

    wait_all(recv_c, c_send)
    wait_all(recv_h, h_send)
    wait_send(x_copies)
    wait_send(g_copies[0])
    wait_send(g_copies[1])


def on_device(tms, rws, latents, hidden, cotangent, conv_one, conv_two, lengths):
    _, fd, rd, cols, ch = latents.shape
    frames, rows = tms * fd, rws * rd
    pix = frames * rows
    local = fd * rd * cols
    group = tms * rws
    flat = lambda x: x.reshape(local, ch)
    vmem = pl.BlockSpec(memory_space=pltpu.VMEM)
    hbm = pl.BlockSpec(memory_space=pltpu.HBM)
    dma = pltpu.SemaphoreType.DMA
    out = pl.pallas_call(
        functools.partial(kernel, (tms, rws, fd, rd, cols, ch)),
        out_shape=jax.ShapeDtypeStruct((pix * ch // 128, 128), F32),
        in_specs=[pl.BlockSpec(memory_space=pltpu.SMEM), vmem, vmem, vmem, hbm, hbm],
        out_specs=vmem,
        scratch_shapes=[
            pltpu.VMEM(conv_two.shape, BF16),
            pltpu.VMEM(conv_one.shape, BF16),
            pltpu.VMEM((ch // 128, local, 128), F32),
            pltpu.VMEM((pix, ch), F32),
            pltpu.VMEM((group, fd * rd, ch), BF16),
            pltpu.VMEM((group, 2 * fd * rd, ch), BF16),
            pltpu.VMEM((group, fd * rd, ch), BF16),
            pltpu.VMEM((group, 2 * fd * rd, ch), BF16),
            pltpu.VMEM((3, pix + 2 * rows, ch), BF16),
            pltpu.VMEM((3, pix + 2 * rows, ch), BF16),
            pltpu.VMEM((pix, 3 * ch), F32),
            pltpu.VMEM((pix, ch), F32),
            pltpu.VMEM((pix, ch), F32),
            dma((2, 3)),
            dma,
            dma,
            dma,
            dma,
            dma((3,)),
            dma((3,)),
            dma((3,)),
            dma((3,)),
            dma((3,)),
            dma((3,)),
        ],
        compiler_params=pltpu.CompilerParams(
            collective_id=0, has_side_effects=True, vmem_limit_bytes=56 * 1024 * 1024
        ),
        name="column_block",
    )(lengths, flat(cotangent), flat(hidden), flat(latents), conv_two, conv_one)
    return out.reshape(1, frames, rows, 1, ch)


def solution(mesh):
    in_specs = (
        P("dp", "tm", "rows", None, None),
        P("dp", "tm", "rows", None, None),
        P("dp", "tm", "rows", None, None),
        P(),
        P(),
        P("dp"),
    )
    out_specs = P("dp", None, None, ("tm", "rows"), None)
    return jax.shard_map(
        functools.partial(on_device, mesh.shape["tm"], mesh.shape["rows"]),
        mesh=mesh,
        in_specs=in_specs,
        out_specs=out_specs,
        check_vma=False,
    )
```

```python
import functools

import jax
import jax.numpy as jnp
from jax import lax
from jax.experimental import pallas as pl
from jax.experimental.pallas import tpu as pltpu
from jax.sharding import PartitionSpec as P

MESH = pl.DeviceIdType.MESH
NT = (((1,), (1,)), ((), ()))
F32 = jnp.float32
BF16 = jnp.bfloat16
SPLIT = 256


def silu_slope(values):
    gate = 1.0 / (1.0 + jnp.exp(-values))
    return gate * (1.0 + values * (1.0 - gate))


def kernel(
    sizes,
    len_ref,
    cot_ref,
    hid_ref,
    lat_ref,
    w_two,
    w_one,
    out_ref,
    wv_two,
    wv_one,
    cot_in,
    hid_in,
    lat_in,
    tmp,
    tmp_back,
    stage_c,
    stage_h,
    stage_l,
    recv_c,
    recv_h,
    recv_l,
    cots,
    grads,
    acc,
    slope_h,
    slope_l,
    in_sem,
    w_sem,
    c_send,
    c_recv,
    h_send,
    h_recv,
    l_send,
    l_recv,
    x_send,
    x_recv,
    ga_send,
    ga_recv,
    gb_send,
    gb_recv,
):
    tms, rws, fd, rd, cols, ch = sizes
    group = tms * rws
    frames = tms * fd
    rows = rws * rd
    pix = frames * rows
    dp = lax.axis_index("dp")
    tm = lax.axis_index("tm")
    rw = lax.axis_index("rows")
    me = tm * rws + rw

    def each_peer(action):
        for step in sorted(range(tms), key=lambda s: -min(s, tms - s)):

            def one(k, carry, step=step):
                turn = k if step == 0 else lax.rem(k + rws // 2 - 1, rws)
                action(lax.rem(tm + step, tms), lax.rem(rw + turn, rws))
                return carry

            lax.fori_loop(1 if step == 0 else 0, rws, one, 0)

    own_copies = []
    for n, (src, dst) in enumerate(((cot_ref, cot_in), (hid_ref, hid_in), (lat_ref, lat_in))):
        own_copies.append(pltpu.make_async_copy(src, dst, in_sem.at[n]))
    own_copies[0].start()

    barrier = pltpu.get_barrier_semaphore()
    each_peer(
        lambda d_tm, d_rw: pl.semaphore_signal(
            barrier, inc=1, device_id=(dp, d_tm, d_rw), device_id_type=MESH
        )
    )

    own_copies[1].start()
    own_copies[2].start()
    weight_copies = []
    for n, (src, dst) in enumerate(((w_two, wv_two), (w_one, wv_one))):
        for at, c in enumerate((1, 0, 2)):
            copy = pltpu.make_async_copy(src.at[:, :, c], dst.at[:, :, c], w_sem.at[n, at])
            copy.start()
            weight_copies.append(copy)

    lanes = out_ref.shape[1]
    strips = ch // lanes
    row_of = lax.broadcasted_iota(jnp.int32, (fd * rd, lanes), 0)
    live = tm * fd + row_of // rd < len_ref[0]

    def columns_of(src_ref, dst_ref, masked):
        for j in range(strips):
            tmp[j] = src_ref[:, j * lanes : (j + 1) * lanes].astype(F32)

        def one(w, carry):
            for j in range(strips):
                block = tmp.at[j][pl.ds(w, fd * rd, stride=cols), :]
                if masked:
                    block = jnp.where(live, block, 0.0)
                dst_ref[w, :, j * lanes : (j + 1) * lanes] = block.astype(BF16)
            return carry

        lax.fori_loop(0, cols, one, 0)

    def send_all(stage, recv, send_sem, recv_sem):
        each_peer(
            lambda d_tm, d_rw: pltpu.make_async_remote_copy(
                src_ref=stage.at[d_tm * rws + d_rw],
                dst_ref=recv.at[me],
                send_sem=send_sem,
                recv_sem=recv_sem,
                device_id=(dp, d_tm, d_rw),
                device_id_type=MESH,
            ).start()
        )

    def wait_all(recv, sem):
        part = recv.at[pl.ds(0, group - 1)]
        pltpu.make_async_copy(part, part, sem).wait()

    own_copies[0].wait()
    columns_of(cot_in, stage_c, True)
    pl.semaphore_wait(barrier, group - 1)
    send_all(stage_c, recv_c, c_send, c_recv)
    own_copies[1].wait()
    columns_of(hid_in, stage_h, False)
    send_all(stage_h, recv_h, h_send, h_recv)
    own_copies[2].wait()
    columns_of(lat_in, stage_l, False)
    recv_c[pl.ds(me, 1)] = stage_c[pl.ds(me, 1)]
    recv_h[pl.ds(me, 1)] = stage_h[pl.ds(me, 1)]
    recv_l[pl.ds(me, 1)] = stage_l[pl.ds(me, 1)]

    tail = cots.shape[1] - pix
    for buf in (cots, grads):
        buf[:, pl.ds(pix, tail), :] = jnp.zeros((3, tail, ch), BF16)

        @pl.when(me == 0)
        def _():
            buf[2, pl.ds(0, pix), :] = jnp.zeros((pix, ch), BF16)

        @pl.when(me == group - 1)
        def _():
            buf[0, pl.ds(0, pix), :] = jnp.zeros((pix, ch), BF16)

    def gather_rows(recv):
        for t in range(tms):
            for pair in range(rws // 2):
                one = recv[t * rws + 2 * pair].astype(F32)
                two = recv[t * rws + 2 * pair + 1].astype(F32)
                for f in range(fd):
                    joined = jnp.concatenate([one[f * rd : (f + 1) * rd], two[f * rd : (f + 1) * rd]], axis=0)
                    start = (t * fd + f) * rows + 2 * pair * rd
                    tmp_back[start : start + 2 * rd, :] = joined

    def to_neighbours(buf, chans, send_sem, recv_sem):
        copies = []
        for to, has, slot in ((me + 1, me < group - 1, 2), (me - 1, me > 0, 0)):
            to = lax.rem(to + group, group)
            copies.append((
                has,
                pltpu.make_async_remote_copy(
                    src_ref=buf.at[1, pl.ds(0, pix), chans],
                    dst_ref=buf.at[slot, pl.ds(0, pix), chans],
                    send_sem=send_sem.at[slot],
                    recv_sem=recv_sem.at[slot],
                    device_id=(dp, to // rws, lax.rem(to, rws)),
                    device_id_type=MESH,
                ),
            ))
        for has, copy in copies:
            pl.when(has)(copy.start)
        return copies

    def wait_recv(copies):
        pl.when(me > 0)(copies[0][1].wait_recv)
        pl.when(me < group - 1)(copies[1][1].wait_recv)

    def wait_send(copies):
        for has, copy in copies:
            pl.when(has)(copy.wait_send)

    wait_all(recv_c, c_recv)
    gather_rows(recv_c)
    cots[1, pl.ds(0, pix), :] = tmp_back[...].astype(BF16)
    x_copies = to_neighbours(cots, pl.ds(0, ch), x_send, x_recv)

    def stacked(buf, columns, ins):
        parts = [buf[c, (2 - a) * rows : (2 - a) * rows + pix, ins] for c in columns for a in range(3)]
        return jnp.concatenate(parts, axis=1)

    def weights(wv, columns, outs, ins):
        return jnp.concatenate(
            [
                jnp.concatenate([wv[a, r, c, outs, ins] for c in columns for a in range(3)], axis=1)
                for r in range(3)
            ],
            axis=0,
        )

    def product(buf, wv, columns, outs, ins):
        return lax.dot_general(
            stacked(buf, columns, ins), weights(wv, columns, outs, ins), NT, preferred_element_type=F32
        )

    every = slice(0, ch)

    def row_taps(above, same, below):
        at_row = lax.rem(lax.broadcasted_iota(jnp.int32, above.shape, 0), rows)
        up = jnp.where(at_row == rows - 1, 0.0, pltpu.roll(above, pix - 1, 0))
        down = jnp.where(at_row == 0, 0.0, pltpu.roll(below, 1, 0))
        return same + up + down

    weight_copies[0].wait()
    acc[...] = product(cots, wv_two, (1,), every, every)
    send_all(stage_l, recv_l, l_send, l_recv)

    wait_all(recv_h, h_recv)
    gather_rows(recv_h)
    slope_h[...] = silu_slope(tmp_back[...])

    weight_copies[1].wait()
    weight_copies[2].wait()
    wait_recv(x_copies)
    g_copies = []
    for outs, send_sem, recv_sem in ((slice(0, SPLIT), ga_send, ga_recv), (slice(SPLIT, ch), gb_send, gb_recv)):
        part = product(cots, wv_two, (0, 2), outs, every)
        n = outs.stop - outs.start
        taps = [
            acc[:, r * ch + outs.start : r * ch + outs.stop] + part[:, r * n : (r + 1) * n] for r in range(3)
        ]
        grads[1, pl.ds(0, pix), outs] = (row_taps(*taps) * slope_h[:, outs]).astype(BF16)
        g_copies.append(to_neighbours(grads, pl.ds(outs.start, n), send_sem, recv_sem))

    weight_copies[3].wait()
    acc[...] = product(grads, wv_one, (1,), every, every)
    wait_all(recv_l, l_recv)
    gather_rows(recv_l)
    slope_l[...] = silu_slope(tmp_back[...])
    weight_copies[4].wait()
    weight_copies[5].wait()
    wait_recv(g_copies[0])
    acc[...] += product(grads, wv_one, (0, 2), every, slice(0, SPLIT))
    wait_recv(g_copies[1])
    part = product(grads, wv_one, (0, 2), every, slice(SPLIT, ch))
    taps = [acc[:, r * ch : (r + 1) * ch] + part[:, r * ch : (r + 1) * ch] for r in range(3)]
    result = cots[1, pl.ds(0, pix), :].astype(F32) + row_taps(*taps) * slope_l[...]
    for j in range(strips):
        out_ref[pl.ds(j, pix, stride=strips), :] = result[:, j * lanes : (j + 1) * lanes]

    wait_all(recv_c, c_send)
    wait_all(recv_h, h_send)
    wait_all(recv_l, l_send)
    wait_send(x_copies)
    wait_send(g_copies[0])
    wait_send(g_copies[1])


def settle(src_ref, dst_ref, sem):
    copy = pltpu.make_async_copy(src_ref, dst_ref, sem)
    copy.start()
    copy.wait()


def on_device(tms, rws, latents, hidden, cotangent, conv_one, conv_two, lengths):
    _, fd, rd, cols, ch = latents.shape
    frames, rows = tms * fd, rws * rd
    pix = frames * rows
    local = fd * rd * cols
    group = tms * rws
    flat = lambda x: x.reshape(local, ch)
    vmem = pl.BlockSpec(memory_space=pltpu.VMEM)
    hbm = pl.BlockSpec(memory_space=pltpu.HBM)
    dma = pltpu.SemaphoreType.DMA
    out = pl.pallas_call(
        functools.partial(kernel, (tms, rws, fd, rd, cols, ch)),
        out_shape=jax.ShapeDtypeStruct((pix * ch // 128, 128), F32),
        in_specs=[pl.BlockSpec(memory_space=pltpu.SMEM), *[hbm] * 5],
        out_specs=vmem,
        scratch_shapes=[
            pltpu.VMEM(conv_two.shape, BF16),
            pltpu.VMEM(conv_one.shape, BF16),
            *[pltpu.VMEM((local, ch), BF16)] * 3,
            pltpu.VMEM((ch // 128, local, 128), F32),
            pltpu.VMEM((pix, ch), F32),
            *[pltpu.VMEM((group, fd * rd, ch), BF16)] * 6,
            pltpu.VMEM((3, pix + 2 * rows, ch), BF16),
            pltpu.VMEM((3, pix + 2 * rows, ch), BF16),
            pltpu.VMEM((pix, 3 * ch), F32),
            pltpu.VMEM((pix, ch), F32),
            pltpu.VMEM((pix, ch), F32),
            dma((3,)),
            dma((2, 3)),
            *[dma] * 6,
            *[dma((3,))] * 6,
        ],
        compiler_params=pltpu.CompilerParams(
            collective_id=0, has_side_effects=True, vmem_limit_bytes=56 * 1024 * 1024
        ),
        name="column_block",
    )(lengths, flat(cotangent), flat(hidden), flat(latents), conv_two, conv_one)
    out = pl.pallas_call(
        settle,
        out_shape=jax.ShapeDtypeStruct(out.shape, F32),
        in_specs=[pl.BlockSpec(memory_space=pl.ANY)],
        out_specs=pl.BlockSpec(memory_space=pl.ANY),
        scratch_shapes=[dma],
        name="settle",
    )(out)
    return out.reshape(1, frames, rows, 1, ch)


def solution(mesh):
    in_specs = (
        P("dp", "tm", "rows", None, None),
        P("dp", "tm", "rows", None, None),
        P("dp", "tm", "rows", None, None),
        P(),
        P(),
        P("dp"),
    )
    out_specs = P("dp", None, None, ("tm", "rows"), None)
    return jax.shard_map(
        functools.partial(on_device, mesh.shape["tm"], mesh.shape["rows"]),
        mesh=mesh,
        in_specs=in_specs,
        out_specs=out_specs,
        check_vma=False,
    )
```

```python
import functools

import jax
import jax.numpy as jnp
from jax import lax
from jax.experimental import pallas as pl
from jax.experimental.pallas import tpu as pltpu
from jax.sharding import PartitionSpec as P

MESH = pl.DeviceIdType.MESH
NT = (((1,), (1,)), ((), ()))
F32 = jnp.float32
BF16 = jnp.bfloat16
SPLIT = 256


def silu_slope(values):
    gate = 1.0 / (1.0 + jnp.exp(-values))
    return gate * (1.0 + values * (1.0 - gate))


def kernel(
    sizes,
    len_ref,
    cot_ref,
    hid_ref,
    lat_ref,
    w_two,
    w_one,
    out_ref,
    masked_out,
    wv_two,
    wv_one,
    cot_in,
    hid_in,
    lat_in,
    tmp,
    tmp_back,
    stage_c,
    stage_h,
    stage_l,
    recv_c,
    recv_h,
    recv_l,
    cots,
    grads,
    acc,
    slope_h,
    slope_l,
    in_sem,
    w_sem,
    c_send,
    c_recv,
    h_send,
    h_recv,
    l_send,
    l_recv,
    x_sem,
    g_sem,
):
    tms, rws, fd, rd, cols, ch = sizes
    group = tms * rws
    frames = tms * fd
    rows = rws * rd
    pix = frames * rows
    dp = lax.axis_index("dp")
    tm = lax.axis_index("tm")
    rw = lax.axis_index("rows")
    me = tm * rws + rw
    odd = lax.rem(rw, 2)
    mate_slot = 2 * odd
    outer_slot = 2 - 2 * odd

    def each_peer(action):
        for step in sorted(range(tms), key=lambda s: -min(s, tms - s)):

            def one(k, carry, step=step):
                turn = k if step == 0 else lax.rem(k + rws // 2 - 1, rws)
                action(lax.rem(tm + step, tms), lax.rem(rw + turn, rws))
                return carry

            lax.fori_loop(1 if step == 0 else 0, rws, one, 0)

    own_copies = []
    for n, (src, dst) in enumerate(((cot_ref, cot_in), (hid_ref, hid_in), (lat_ref, lat_in))):
        own_copies.append(pltpu.make_async_copy(src, dst, in_sem.at[n]))
    own_copies[0].start()

    barrier = pltpu.get_barrier_semaphore()
    each_peer(
        lambda d_tm, d_rw: pl.semaphore_signal(
            barrier, inc=1, device_id=(dp, d_tm, d_rw), device_id_type=MESH
        )
    )

    own_copies[1].start()
    own_copies[2].start()
    weight_copies = []
    for n, (src, dst) in enumerate(((w_two, wv_two), (w_one, wv_one))):
        for at, c in enumerate((1, 0, 2)):
            copy = pltpu.make_async_copy(src.at[:, :, c], dst.at[:, :, c], w_sem.at[n, at])
            copy.start()
            weight_copies.append(copy)

    lanes = out_ref.shape[1]
    strips = ch // lanes
    row_of = lax.broadcasted_iota(jnp.int32, (fd * rd, lanes), 0)
    live = tm * fd + row_of // rd < len_ref[0]

    def columns_of(src_ref, dst_ref, first, masked):
        for j in range(strips):
            tmp[j] = src_ref[:, j * lanes : (j + 1) * lanes].astype(F32)

        def one(w, carry):
            for j in range(strips):
                block = tmp.at[j][pl.ds(w, fd * rd, stride=cols), :]
                if masked:
                    block = jnp.where(live, block, 0.0)
                dst_ref[first + w, :, j * lanes : (j + 1) * lanes] = block.astype(BF16)
            return carry

        lax.fori_loop(0, cols, one, 0)

    def pair_at(device):
        return pl.ds(device + lax.rem(device, 2), 2)

    def send_all(stage, recv, at, send_sem, recv_sem):
        each_peer(
            lambda d_tm, d_rw: pltpu.make_async_remote_copy(
                src_ref=stage.at[at(d_tm * rws + d_rw)],
                dst_ref=recv.at[me],
                send_sem=send_sem,
                recv_sem=recv_sem,
                device_id=(dp, d_tm, d_rw),
                device_id_type=MESH,
            ).start()
        )

    def wait_all(recv, sem):
        part = recv.at[pl.ds(0, group - 1)]
        pltpu.make_async_copy(part, part, sem).wait()

    no_column = jnp.zeros((fd * rd, ch), BF16)
    stage_c[0] = no_column
    stage_c[cols + 1] = no_column
    own_copies[0].wait()
    columns_of(cot_in, stage_c, 1, True)
    pl.semaphore_wait(barrier, group - 1)
    send_all(stage_c, recv_c, pair_at, c_send, c_recv)
    own_copies[1].wait()
    columns_of(hid_in, stage_h, 0, False)
    send_all(stage_h, recv_h, lambda device: device, h_send, h_recv)
    own_copies[2].wait()
    columns_of(lat_in, stage_l, 0, False)
    send_all(stage_l, recv_l, lambda device: device, l_send, l_recv)
    recv_c[me] = stage_c[pair_at(me)]
    recv_h[me] = stage_h[me]
    recv_l[me] = stage_l[me]

    tail = cots.shape[1] - pix
    for buf in (cots, grads):
        buf[:, pl.ds(pix, tail), :] = jnp.zeros((3, tail, ch), BF16)

    @pl.when((me == 0) | (me == group - 1))
    def _():
        grads[outer_slot, pl.ds(0, pix), :] = jnp.zeros((pix, ch), BF16)

    def gather_rows(block):
        for t in range(tms):
            for pair in range(rws // 2):
                one = block(t * rws + 2 * pair).astype(F32)
                two = block(t * rws + 2 * pair + 1).astype(F32)
                for f in range(fd):
                    joined = jnp.concatenate([one[f * rd : (f + 1) * rd], two[f * rd : (f + 1) * rd]], axis=0)
                    start = (t * fd + f) * rows + 2 * pair * rd
                    tmp_back[start : start + 2 * rd, :] = joined

    def copy_column(buf, chans, slot, target, send_sem, recv_sem):
        return pltpu.make_async_remote_copy(
            src_ref=buf.at[1, pl.ds(0, pix), chans],
            dst_ref=buf.at[slot, pl.ds(0, pix), chans],
            send_sem=send_sem,
            recv_sem=recv_sem,
            device_id=(dp, target // rws, lax.rem(target, rws)),
            device_id_type=MESH,
        )

    def to_mate(buf, chans, sems):
        return copy_column(buf, chans, outer_slot, me + 1 - 2 * odd, *sems)

    inner = (me > 0) & (me < group - 1)

    def to_outer(buf, chans, sems):
        return copy_column(buf, chans, mate_slot, lax.rem(me + 2 * odd - 1 + group, group), *sems)

    wait_all(recv_c, c_recv)
    gather_rows(lambda source: recv_c[source, 1 - odd])
    cots[1, pl.ds(0, pix), :] = tmp_back[...].astype(BF16)
    mate_copy = to_mate(cots, pl.ds(0, ch), (x_sem.at[0], x_sem.at[1]))
    mate_copy.start()
    gather_rows(lambda source: recv_c[source, odd])
    cots[outer_slot, pl.ds(0, pix), :] = tmp_back[...].astype(BF16)

    def stacked(buf, columns, ins):
        parts = [buf[c, (2 - a) * rows : (2 - a) * rows + pix, ins] for c in columns for a in range(3)]
        return jnp.concatenate(parts, axis=1)

    def weights(wv, columns, outs, ins):
        return jnp.concatenate(
            [
                jnp.concatenate([wv[a, r, c, outs, ins] for c in columns for a in range(3)], axis=1)
                for r in range(3)
            ],
            axis=0,
        )

    def product(buf, wv, columns, outs, ins):
        return lax.dot_general(
            stacked(buf, columns, ins), weights(wv, columns, outs, ins), NT, preferred_element_type=F32
        )

    every = slice(0, ch)

    def row_taps(above, same, below):
        at_row = lax.rem(lax.broadcasted_iota(jnp.int32, above.shape, 0), rows)
        up = jnp.where(at_row == rows - 1, 0.0, pltpu.roll(above, pix - 1, 0))
        down = jnp.where(at_row == 0, 0.0, pltpu.roll(below, 1, 0))
        return same + up + down

    for copy in weight_copies[:3]:
        copy.wait()
    g_copies = []
    for at, outs in enumerate((slice(0, SPLIT), slice(SPLIT, ch))):
        n = outs.stop - outs.start
        acc[:, : 3 * n] = product(cots, wv_two, (1, outer_slot), outs, every)
        if at == 0:
            wait_all(recv_h, h_recv)
            gather_rows(lambda source: recv_h[source])
            slope_h[...] = silu_slope(tmp_back[...])
            mate_copy.wait_recv()
        part = product(cots, wv_two, (mate_slot,), outs, every)
        taps = [acc[:, r * n : (r + 1) * n] + part[:, r * n : (r + 1) * n] for r in range(3)]
        grads[1, pl.ds(0, pix), outs] = (row_taps(*taps) * slope_h[:, outs]).astype(BF16)
        chans = pl.ds(outs.start, n)
        outer = to_outer(grads, chans, (g_sem.at[at, 0], g_sem.at[at, 1]))
        mate = to_mate(grads, chans, (g_sem.at[at, 2], g_sem.at[at, 3]))
        pl.when(inner)(outer.start)
        mate.start()
        g_copies.append((outer, mate))

    for copy in weight_copies[3:]:
        copy.wait()
    acc[...] = product(grads, wv_one, (1,), every, every)
    masked = cots[1, pl.ds(0, pix), :].astype(F32)
    for j in range(strips):
        masked_out[pl.ds(j, pix, stride=strips), :] = masked[:, j * lanes : (j + 1) * lanes]
    for _, mate in g_copies:
        mate.wait_recv()
    acc[...] += product(grads, wv_one, (mate_slot,), every, every)
    wait_all(recv_l, l_recv)
    gather_rows(lambda source: recv_l[source])
    slope_l[...] = silu_slope(tmp_back[...])
    pl.when(inner)(g_copies[0][0].wait_recv)
    acc[...] += product(grads, wv_one, (outer_slot,), every, slice(0, SPLIT))
    pl.when(inner)(g_copies[1][0].wait_recv)
    part = product(grads, wv_one, (outer_slot,), every, slice(SPLIT, ch))
    taps = [acc[:, r * ch : (r + 1) * ch] + part[:, r * ch : (r + 1) * ch] for r in range(3)]
    result = row_taps(*taps) * slope_l[...]
    for j in range(strips):
        out_ref[pl.ds(j, pix, stride=strips), :] = result[:, j * lanes : (j + 1) * lanes]

    wait_all(recv_c, c_send)
    wait_all(recv_h, h_send)
    wait_all(recv_l, l_send)
    mate_copy.wait_send()
    for outer, mate in g_copies:
        pl.when(inner)(outer.wait_send)
        mate.wait_send()


def on_device(tms, rws, latents, hidden, cotangent, conv_one, conv_two, lengths):
    _, fd, rd, cols, ch = latents.shape
    frames, rows = tms * fd, rws * rd
    pix = frames * rows
    local = fd * rd * cols
    group = tms * rws
    flat = lambda x: x.reshape(local, ch)
    vmem = pl.BlockSpec(memory_space=pltpu.VMEM)
    hbm = pl.BlockSpec(memory_space=pltpu.HBM)
    dma = pltpu.SemaphoreType.DMA
    out, masked = pl.pallas_call(
        functools.partial(kernel, (tms, rws, fd, rd, cols, ch)),
        out_shape=[jax.ShapeDtypeStruct((pix * ch // 128, 128), F32)] * 2,
        in_specs=[pl.BlockSpec(memory_space=pltpu.SMEM), *[hbm] * 5],
        out_specs=[vmem, vmem],
        scratch_shapes=[
            pltpu.VMEM(conv_two.shape, BF16),
            pltpu.VMEM(conv_one.shape, BF16),
            *[pltpu.VMEM((local, ch), BF16)] * 3,
            pltpu.VMEM((ch // 128, local, 128), F32),
            pltpu.VMEM((pix, ch), F32),
            pltpu.VMEM((cols + 2, fd * rd, ch), BF16),
            *[pltpu.VMEM((cols, fd * rd, ch), BF16)] * 2,
            pltpu.VMEM((group, 2, fd * rd, ch), BF16),
            *[pltpu.VMEM((group, fd * rd, ch), BF16)] * 2,
            pltpu.VMEM((3, pix + 2 * rows, ch), BF16),
            pltpu.VMEM((3, pix + 2 * rows, ch), BF16),
            pltpu.VMEM((pix, 3 * ch), F32),
            pltpu.VMEM((pix, ch), F32),
            pltpu.VMEM((pix, ch), F32),
            dma((3,)),
            dma((2, 3)),
            *[dma] * 6,
            dma((2,)),
            dma((2, 4)),
        ],
        compiler_params=pltpu.CompilerParams(
            collective_id=0, has_side_effects=True, vmem_limit_bytes=56 * 1024 * 1024
        ),
        name="column_block",
    )(lengths, flat(cotangent), flat(hidden), flat(latents), conv_two, conv_one)
    out = masked + out
    return out.reshape(1, frames, rows, 1, ch)


def solution(mesh):
    in_specs = (
        P("dp", "tm", "rows", None, None),
        P("dp", "tm", "rows", None, None),
        P("dp", "tm", "rows", None, None),
        P(),
        P(),
        P("dp"),
    )
    out_specs = P("dp", None, None, ("tm", "rows"), None)
    return jax.shard_map(
        functools.partial(on_device, mesh.shape["tm"], mesh.shape["rows"]),
        mesh=mesh,
        in_specs=in_specs,
        out_specs=out_specs,
        check_vma=False,
    )
```

```python
import functools

import jax
import jax.numpy as jnp
from jax import lax
from jax.experimental import pallas as pl
from jax.experimental.pallas import tpu as pltpu
from jax.sharding import PartitionSpec as P

MESH = pl.DeviceIdType.MESH
NT = (((1,), (1,)), ((), ()))
F32 = jnp.float32
BF16 = jnp.bfloat16
SPLIT = 256


def silu_slope(values):
    gate = 1.0 / (1.0 + jnp.exp(-values))
    return gate * (1.0 + values * (1.0 - gate))


def kernel(
    sizes,
    len_ref,
    cot_ref,
    hid_ref,
    lat_ref,
    w_two,
    w_one,
    out_ref,
    wv_two,
    wv_one,
    cot_in,
    hid_in,
    lat_in,
    tmp,
    tmp_back,
    stage_c,
    stage_h,
    stage_l,
    recv_c,
    recv_h,
    recv_l,
    cots,
    grads,
    acc,
    slope_h,
    slope_l,
    in_sem,
    w_sem,
    c_send,
    c_recv,
    h_send,
    h_recv,
    l_send,
    l_recv,
    x_sem,
    g_sem,
):
    tms, rws, fd, rd, cols, ch = sizes
    group = tms * rws
    frames = tms * fd
    rows = rws * rd
    pix = frames * rows
    dp = lax.axis_index("dp")
    tm = lax.axis_index("tm")
    rw = lax.axis_index("rows")
    me = tm * rws + rw
    odd = lax.rem(rw, 2)
    mate_slot = 2 * odd
    outer_slot = 2 - 2 * odd

    def each_peer(action):
        for step in sorted(range(tms), key=lambda s: -min(s, tms - s)):

            def one(k, carry, step=step):
                turn = k if step == 0 else lax.rem(k + rws // 2 - 1, rws)
                action(lax.rem(tm + step, tms), lax.rem(rw + turn, rws))
                return carry

            lax.fori_loop(1 if step == 0 else 0, rws, one, 0)

    own_copies = []
    for n, (src, dst) in enumerate(((cot_ref, cot_in), (hid_ref, hid_in), (lat_ref, lat_in))):
        own_copies.append(pltpu.make_async_copy(src, dst, in_sem.at[n]))
    own_copies[0].start()

    barrier = pltpu.get_barrier_semaphore()
    each_peer(
        lambda d_tm, d_rw: pl.semaphore_signal(
            barrier, inc=1, device_id=(dp, d_tm, d_rw), device_id_type=MESH
        )
    )

    own_copies[1].start()
    own_copies[2].start()
    weight_copies = []
    for n, (src, dst) in enumerate(((w_two, wv_two), (w_one, wv_one))):
        for at, c in enumerate((1, 0, 2)):
            copy = pltpu.make_async_copy(src.at[:, :, c], dst.at[:, :, c], w_sem.at[n, at])
            copy.start()
            weight_copies.append(copy)

    lanes = out_ref.shape[1]
    strips = ch // lanes
    row_of = lax.broadcasted_iota(jnp.int32, (fd * rd, lanes), 0)
    live = tm * fd + row_of // rd < len_ref[0]

    def columns_of(src_ref, dst_ref, first, masked):
        for j in range(strips):
            tmp[j] = src_ref[:, j * lanes : (j + 1) * lanes].astype(F32)

        def one(w, carry):
            for j in range(strips):
                block = tmp.at[j][pl.ds(w, fd * rd, stride=cols), :]
                if masked:
                    block = jnp.where(live, block, 0.0)
                dst_ref[first + w, :, j * lanes : (j + 1) * lanes] = block.astype(BF16)
            return carry

        lax.fori_loop(0, cols, one, 0)

    def pair_at(device):
        return pl.ds(device + lax.rem(device, 2), 2)

    def send_all(stage, recv, at, send_sem, recv_sem):
        each_peer(
            lambda d_tm, d_rw: pltpu.make_async_remote_copy(
                src_ref=stage.at[at(d_tm * rws + d_rw)],
                dst_ref=recv.at[me],
                send_sem=send_sem,
                recv_sem=recv_sem,
                device_id=(dp, d_tm, d_rw),
                device_id_type=MESH,
            ).start()
        )

    def wait_all(recv, sem):
        part = recv.at[pl.ds(0, group - 1)]
        pltpu.make_async_copy(part, part, sem).wait()

    no_column = jnp.zeros((fd * rd, ch), BF16)
    stage_c[0] = no_column
    stage_c[cols + 1] = no_column
    own_copies[0].wait()
    columns_of(cot_in, stage_c, 1, True)
    pl.semaphore_wait(barrier, group - 1)
    send_all(stage_c, recv_c, pair_at, c_send, c_recv)
    own_copies[1].wait()
    columns_of(hid_in, stage_h, 0, False)
    send_all(stage_h, recv_h, lambda device: device, h_send, h_recv)
    own_copies[2].wait()
    columns_of(lat_in, stage_l, 0, False)
    send_all(stage_l, recv_l, lambda device: device, l_send, l_recv)
    recv_c[me] = stage_c[pair_at(me)]
    recv_h[me] = stage_h[me]
    recv_l[me] = stage_l[me]

    tail = cots.shape[1] - pix
    for buf in (cots, grads):
        buf[:, pl.ds(pix, tail), :] = jnp.zeros((3, tail, ch), BF16)

    @pl.when((me == 0) | (me == group - 1))
    def _():
        grads[outer_slot, pl.ds(0, pix), :] = jnp.zeros((pix, ch), BF16)

    def gather_rows(block):
        for t in range(tms):
            for pair in range(rws // 2):
                one = block(t * rws + 2 * pair).astype(F32)
                two = block(t * rws + 2 * pair + 1).astype(F32)
                for f in range(fd):
                    joined = jnp.concatenate([one[f * rd : (f + 1) * rd], two[f * rd : (f + 1) * rd]], axis=0)
                    start = (t * fd + f) * rows + 2 * pair * rd
                    tmp_back[start : start + 2 * rd, :] = joined

    def copy_column(buf, chans, slot, target, send_sem, recv_sem):
        return pltpu.make_async_remote_copy(
            src_ref=buf.at[1, pl.ds(0, pix), chans],
            dst_ref=buf.at[slot, pl.ds(0, pix), chans],
            send_sem=send_sem,
            recv_sem=recv_sem,
            device_id=(dp, target // rws, lax.rem(target, rws)),
            device_id_type=MESH,
        )

    def to_mate(buf, chans, sems):
        return copy_column(buf, chans, outer_slot, me + 1 - 2 * odd, *sems)

    inner = (me > 0) & (me < group - 1)

    def to_outer(buf, chans, sems):
        return copy_column(buf, chans, mate_slot, lax.rem(me + 2 * odd - 1 + group, group), *sems)

    wait_all(recv_c, c_recv)
    gather_rows(lambda source: recv_c[source, 1 - odd])
    cots[1, pl.ds(0, pix), :] = tmp_back[...].astype(BF16)
    mate_copy = to_mate(cots, pl.ds(0, ch), (x_sem.at[0], x_sem.at[1]))
    mate_copy.start()
    gather_rows(lambda source: recv_c[source, odd])
    cots[outer_slot, pl.ds(0, pix), :] = tmp_back[...].astype(BF16)

    def stacked(buf, columns, ins):
        parts = [buf[c, (2 - a) * rows : (2 - a) * rows + pix, ins] for c in columns for a in range(3)]
        return jnp.concatenate(parts, axis=1)

    def weights(wv, columns, outs, ins):
        return jnp.concatenate(
            [
                jnp.concatenate([wv[a, r, c, outs, ins] for c in columns for a in range(3)], axis=1)
                for r in range(3)
            ],
            axis=0,
        )

    def product(buf, wv, columns, outs, ins):
        return lax.dot_general(
            stacked(buf, columns, ins), weights(wv, columns, outs, ins), NT, preferred_element_type=F32
        )

    every = slice(0, ch)

    def row_taps(above, same, below):
        at_row = lax.rem(lax.broadcasted_iota(jnp.int32, above.shape, 0), rows)
        up = jnp.where(at_row == rows - 1, 0.0, pltpu.roll(above, pix - 1, 0))
        down = jnp.where(at_row == 0, 0.0, pltpu.roll(below, 1, 0))
        return same + up + down

    for copy in weight_copies[:3]:
        copy.wait()
    g_copies = []
    for at, outs in enumerate((slice(0, SPLIT), slice(SPLIT, ch))):
        n = outs.stop - outs.start
        acc[:, : 3 * n] = product(cots, wv_two, (1, outer_slot), outs, every)
        if at == 0:
            wait_all(recv_h, h_recv)
            gather_rows(lambda source: recv_h[source])
            slope_h[...] = silu_slope(tmp_back[...])
            mate_copy.wait_recv()
        part = product(cots, wv_two, (mate_slot,), outs, every)
        taps = [acc[:, r * n : (r + 1) * n] + part[:, r * n : (r + 1) * n] for r in range(3)]
        grads[1, pl.ds(0, pix), outs] = (row_taps(*taps) * slope_h[:, outs]).astype(BF16)
        chans = pl.ds(outs.start, n)
        outer = to_outer(grads, chans, (g_sem.at[at, 0], g_sem.at[at, 1]))
        mate = to_mate(grads, chans, (g_sem.at[at, 2], g_sem.at[at, 3]))
        pl.when(inner)(outer.start)
        mate.start()
        g_copies.append((outer, mate))

    for copy in weight_copies[3:]:
        copy.wait()
    acc[...] = product(grads, wv_one, (1,), every, every)
    for _, mate in g_copies:
        mate.wait_recv()
    acc[...] += product(grads, wv_one, (mate_slot,), every, every)
    wait_all(recv_l, l_recv)
    gather_rows(lambda source: recv_l[source])
    slope_l[...] = silu_slope(tmp_back[...])
    pl.when(inner)(g_copies[0][0].wait_recv)
    acc[...] += product(grads, wv_one, (outer_slot,), every, slice(0, SPLIT))
    pl.when(inner)(g_copies[1][0].wait_recv)
    part = product(grads, wv_one, (outer_slot,), every, slice(SPLIT, ch))
    taps = [acc[:, r * ch : (r + 1) * ch] + part[:, r * ch : (r + 1) * ch] for r in range(3)]
    result = cots[1, pl.ds(0, pix), :].astype(F32) + row_taps(*taps) * slope_l[...]
    for j in range(strips):
        out_ref[pl.ds(j, pix, stride=strips), :] = result[:, j * lanes : (j + 1) * lanes]

    wait_all(recv_c, c_send)
    wait_all(recv_h, h_send)
    wait_all(recv_l, l_send)
    mate_copy.wait_send()
    for outer, mate in g_copies:
        pl.when(inner)(outer.wait_send)
        mate.wait_send()


def on_device(tms, rws, latents, hidden, cotangent, conv_one, conv_two, lengths):
    _, fd, rd, cols, ch = latents.shape
    frames, rows = tms * fd, rws * rd
    pix = frames * rows
    local = fd * rd * cols
    group = tms * rws
    in_hbm = lambda x: pltpu.with_memory_space_constraint(x, pltpu.HBM)
    flat = lambda x: in_hbm(x.reshape(local, ch))
    vmem = pl.BlockSpec(memory_space=pltpu.VMEM)
    hbm = pl.BlockSpec(memory_space=pltpu.HBM)
    dma = pltpu.SemaphoreType.DMA
    out = pl.pallas_call(
        functools.partial(kernel, (tms, rws, fd, rd, cols, ch)),
        out_shape=jax.ShapeDtypeStruct((pix * ch // 128, 128), F32),
        in_specs=[pl.BlockSpec(memory_space=pltpu.SMEM), *[hbm] * 5],
        out_specs=vmem,
        scratch_shapes=[
            pltpu.VMEM(conv_two.shape, BF16),
            pltpu.VMEM(conv_one.shape, BF16),
            *[pltpu.VMEM((local, ch), BF16)] * 3,
            pltpu.VMEM((ch // 128, local, 128), F32),
            pltpu.VMEM((pix, ch), F32),
            pltpu.VMEM((cols + 2, fd * rd, ch), BF16),
            *[pltpu.VMEM((cols, fd * rd, ch), BF16)] * 2,
            pltpu.VMEM((group, 2, fd * rd, ch), BF16),
            *[pltpu.VMEM((group, fd * rd, ch), BF16)] * 2,
            pltpu.VMEM((3, pix + 2 * rows, ch), BF16),
            pltpu.VMEM((3, pix + 2 * rows, ch), BF16),
            pltpu.VMEM((pix, 3 * ch), F32),
            pltpu.VMEM((pix, ch), F32),
            pltpu.VMEM((pix, ch), F32),
            dma((3,)),
            dma((2, 3)),
            *[dma] * 6,
            dma((2,)),
            dma((2, 4)),
        ],
        compiler_params=pltpu.CompilerParams(
            collective_id=0, has_side_effects=True, vmem_limit_bytes=50 * 1024 * 1024
        ),
        name="column_block",
    )(lengths, flat(cotangent), flat(hidden), flat(latents), in_hbm(conv_two), in_hbm(conv_one))
    return out.reshape(1, frames, rows, 1, ch)


def solution(mesh):
    in_specs = (
        P("dp", "tm", "rows", None, None),
        P("dp", "tm", "rows", None, None),
        P("dp", "tm", "rows", None, None),
        P(),
        P(),
        P("dp"),
    )
    out_specs = P("dp", None, None, ("tm", "rows"), None)
    return jax.shard_map(
        functools.partial(on_device, mesh.shape["tm"], mesh.shape["rows"]),
        mesh=mesh,
        in_specs=in_specs,
        out_specs=out_specs,
        check_vma=False,
    )
```

```python
import functools

import jax
import jax.numpy as jnp
from jax import lax
from jax.experimental import pallas as pl
from jax.experimental.pallas import tpu as pltpu
from jax.sharding import PartitionSpec as P

MESH = pl.DeviceIdType.MESH
NT = (((1,), (1,)), ((), ()))
F32 = jnp.float32
BF16 = jnp.bfloat16
SPLIT = 256


def silu_slope(values):
    gate = 1.0 / (1.0 + jnp.exp(-values))
    return gate * (1.0 + values * (1.0 - gate))


def kernel(
    sizes,
    len_ref,
    cot_ref,
    hid_ref,
    lat_ref,
    w_two,
    w_one,
    out_ref,
    wv_two,
    wv_one,
    cot_in,
    hid_in,
    lat_in,
    tmp,
    stage_c,
    stage_h,
    stage_l,
    recv_c,
    recv_o,
    recv_h,
    recv_l,
    cots,
    grads,
    acc,
    slope_h,
    slope_l,
    in_sem,
    w_sem,
    c_send,
    c_recv,
    o_send,
    o_recv,
    h_send,
    h_recv,
    l_send,
    l_recv,
    x_sem,
    g_sem,
):
    tms, rws, fd, rd, cols, ch = sizes
    group = tms * rws
    frames = tms * fd
    rows = rws * rd
    pix = frames * rows
    dp = lax.axis_index("dp")
    tm = lax.axis_index("tm")
    rw = lax.axis_index("rows")
    me = tm * rws + rw
    odd = lax.rem(rw, 2)
    mate_slot = 2 * odd
    outer_slot = 2 - 2 * odd

    def each_peer(action):
        for step in sorted(range(tms), key=lambda s: -min(s, tms - s)):

            def one(k, carry, step=step):
                turn = k if step == 0 else lax.rem(k + rws // 2 - 1, rws)
                action(lax.rem(tm + step, tms), lax.rem(rw + turn, rws))
                return carry

            lax.fori_loop(1 if step == 0 else 0, rws, one, 0)

    own_copies = []
    for n, (src, dst) in enumerate(((cot_ref, cot_in), (hid_ref, hid_in), (lat_ref, lat_in))):
        own_copies.append(pltpu.make_async_copy(src, dst, in_sem.at[n]))
    own_copies[0].start()

    barrier = pltpu.get_barrier_semaphore()
    each_peer(
        lambda d_tm, d_rw: pl.semaphore_signal(
            barrier, inc=1, device_id=(dp, d_tm, d_rw), device_id_type=MESH
        )
    )

    own_copies[1].start()
    own_copies[2].start()
    weight_copies = []
    for n, (src, dst) in enumerate(((w_two, wv_two), (w_one, wv_one))):
        for at, c in enumerate((1, 0, 2)):
            copy = pltpu.make_async_copy(src.at[:, :, c], dst.at[:, :, c], w_sem.at[n, at])
            copy.start()
            weight_copies.append(copy)

    lanes = out_ref.shape[1]
    strips = ch // lanes
    row_of = lax.broadcasted_iota(jnp.int32, (fd * rd, lanes), 0)
    live = tm * fd + row_of // rd < len_ref[0]

    def columns_of(src_ref, dst_ref, first, masked):
        for j in range(strips):
            tmp[j] = src_ref[:, j * lanes : (j + 1) * lanes].astype(F32)

        def one(w, carry):
            for j in range(strips):
                block = tmp.at[j][pl.ds(w, fd * rd, stride=cols), :]
                if masked:
                    block = jnp.where(live, block, 0.0)
                dst_ref[first + w, :, j * lanes : (j + 1) * lanes] = block.astype(BF16)
            return carry

        lax.fori_loop(0, cols, one, 0)

    def outer_at(device):
        return device + 2 * lax.rem(device, 2)

    def send_all(stage, recv, at, send_sem, recv_sem, chans=None):
        chans = pl.ds(0, ch) if chans is None else chans

        each_peer(
            lambda d_tm, d_rw: pltpu.make_async_remote_copy(
                src_ref=stage.at[at(d_tm * rws + d_rw), :, chans],
                dst_ref=recv.at[me, :, chans],
                send_sem=send_sem,
                recv_sem=recv_sem,
                device_id=(dp, d_tm, d_rw),
                device_id_type=MESH,
            ).start()
        )

    def wait_all(recv, sem, chans=None):
        part = recv.at[pl.ds(0, group - 1), :, pl.ds(0, ch) if chans is None else chans]
        pltpu.make_async_copy(part, part, sem).wait()

    no_column = jnp.zeros((fd * rd, ch), BF16)
    stage_c[0] = no_column
    stage_c[cols + 1] = no_column
    blocks = (pl.ds(0, SPLIT), pl.ds(SPLIT, ch - SPLIT))
    own_copies[0].wait()
    columns_of(cot_in, stage_c, 1, True)
    pl.semaphore_wait(barrier, group - 1)
    send_all(stage_c, recv_c, lambda device: device + 1, c_send, c_recv)
    send_all(stage_c, recv_o, outer_at, o_send, o_recv)
    own_copies[1].wait()
    columns_of(hid_in, stage_h, 0, False)
    for at, chans in enumerate(blocks):
        send_all(stage_h, recv_h, lambda device: device, h_send.at[at], h_recv.at[at], chans)
    own_copies[2].wait()
    columns_of(lat_in, stage_l, 0, False)
    send_all(stage_l, recv_l, lambda device: device, l_send, l_recv)
    recv_c[me] = stage_c[me + 1]
    recv_o[me] = stage_c[outer_at(me)]
    recv_h[me] = stage_h[me]
    recv_l[me] = stage_l[me]

    tail = cots.shape[1] - pix
    for buf in (cots, grads):
        buf[:, pl.ds(pix, tail), :] = jnp.zeros((3, tail, ch), BF16)

    @pl.when((me == 0) | (me == group - 1))
    def _():
        grads[outer_slot, pl.ds(0, pix), :] = jnp.zeros((pix, ch), BF16)

    def gather_rows(recv, write, chans=slice(None)):
        for t in range(tms):
            for f in range(fd):
                for first in range(0, rws, 4):
                    parts = [recv[t * rws + first + i, f * rd : (f + 1) * rd, chans] for i in range(4)]
                    write(pl.ds((t * fd + f) * rows + first * rd, 4 * rd), chans, jnp.concatenate(parts, axis=0))

    def into(buf, slot):
        def write(at, chans, block):
            buf[slot, at, chans] = block

        return write

    def slope_into(buf):
        def write(at, chans, block):
            buf[at, chans] = silu_slope(block.astype(F32))

        return write

    def copy_column(buf, chans, slot, target, send_sem, recv_sem):
        return pltpu.make_async_remote_copy(
            src_ref=buf.at[1, pl.ds(0, pix), chans],
            dst_ref=buf.at[slot, pl.ds(0, pix), chans],
            send_sem=send_sem,
            recv_sem=recv_sem,
            device_id=(dp, target // rws, lax.rem(target, rws)),
            device_id_type=MESH,
        )

    def to_mate(buf, chans, sems):
        return copy_column(buf, chans, outer_slot, me + 1 - 2 * odd, *sems)

    inner = (me > 0) & (me < group - 1)

    def to_outer(buf, chans, sems):
        return copy_column(buf, chans, mate_slot, lax.rem(me + 2 * odd - 1 + group, group), *sems)

    wait_all(recv_c, c_recv)
    gather_rows(recv_c, into(cots, 1))
    mate_copy = to_mate(cots, pl.ds(0, ch), (x_sem.at[0], x_sem.at[1]))
    mate_copy.start()

    def stacked(buf, columns, ins):
        parts = [buf[c, (2 - a) * rows : (2 - a) * rows + pix, ins] for c in columns for a in range(3)]
        return jnp.concatenate(parts, axis=1)

    def weights(wv, columns, outs, ins):
        return jnp.concatenate(
            [
                jnp.concatenate([wv[a, r, c, outs, ins] for c in columns for a in range(3)], axis=1)
                for r in range(3)
            ],
            axis=0,
        )

    def product(buf, wv, columns, outs, ins):
        return lax.dot_general(
            stacked(buf, columns, ins), weights(wv, columns, outs, ins), NT, preferred_element_type=F32
        )

    every = slice(0, ch)

    def row_taps(above, same, below):
        at_row = lax.rem(lax.broadcasted_iota(jnp.int32, above.shape, 0), rows)
        up = jnp.where(at_row == rows - 1, 0.0, pltpu.roll(above, pix - 1, 0))
        down = jnp.where(at_row == 0, 0.0, pltpu.roll(below, 1, 0))
        return same + up + down

    weight_copies[0].wait()
    acc[...] = product(cots, wv_two, (1,), every, every)
    wait_all(recv_o, o_recv)
    gather_rows(recv_o, into(cots, outer_slot))
    for copy in weight_copies[1:3]:
        copy.wait()
    mate_copy.wait_recv()
    g_copies = []
    for at, outs in enumerate((slice(0, SPLIT), slice(SPLIT, ch))):
        n = outs.stop - outs.start
        part = product(cots, wv_two, (mate_slot, outer_slot), outs, every)
        taps = [acc[:, r * ch + outs.start : r * ch + outs.stop] + part[:, r * n : (r + 1) * n] for r in range(3)]
        wait_all(recv_h, h_recv.at[at], blocks[at])
        gather_rows(recv_h, slope_into(slope_h), outs)
        grads[1, pl.ds(0, pix), outs] = (row_taps(*taps) * slope_h[:, outs]).astype(BF16)
        chans = pl.ds(outs.start, n)
        outer = to_outer(grads, chans, (g_sem.at[at, 0], g_sem.at[at, 1]))
        mate = to_mate(grads, chans, (g_sem.at[at, 2], g_sem.at[at, 3]))
        pl.when(inner)(outer.start)
        mate.start()
        g_copies.append((outer, mate))

    for copy in weight_copies[3:]:
        copy.wait()
    acc[...] = product(grads, wv_one, (1,), every, every)
    for _, mate in g_copies:
        mate.wait_recv()
    acc[...] += product(grads, wv_one, (mate_slot,), every, every)
    wait_all(recv_l, l_recv)
    gather_rows(recv_l, slope_into(slope_l))
    pl.when(inner)(g_copies[0][0].wait_recv)
    acc[...] += product(grads, wv_one, (outer_slot,), every, slice(0, SPLIT))
    pl.when(inner)(g_copies[1][0].wait_recv)
    part = product(grads, wv_one, (outer_slot,), every, slice(SPLIT, ch))
    taps = [acc[:, r * ch : (r + 1) * ch] + part[:, r * ch : (r + 1) * ch] for r in range(3)]
    result = cots[1, pl.ds(0, pix), :].astype(F32) + row_taps(*taps) * slope_l[...]
    for j in range(strips):
        out_ref[pl.ds(j, pix, stride=strips), :] = result[:, j * lanes : (j + 1) * lanes]

    wait_all(recv_c, c_send)
    wait_all(recv_o, o_send)
    for at, chans in enumerate(blocks):
        wait_all(recv_h, h_send.at[at], chans)
    wait_all(recv_l, l_send)
    mate_copy.wait_send()
    for outer, mate in g_copies:
        pl.when(inner)(outer.wait_send)
        mate.wait_send()


def on_device(tms, rws, latents, hidden, cotangent, conv_one, conv_two, lengths):
    _, fd, rd, cols, ch = latents.shape
    frames, rows = tms * fd, rws * rd
    pix = frames * rows
    local = fd * rd * cols
    group = tms * rws
    in_hbm = lambda x: pltpu.with_memory_space_constraint(x, pltpu.HBM)
    flat = lambda x: in_hbm(x.reshape(local, ch))
    vmem = pl.BlockSpec(memory_space=pltpu.VMEM)
    hbm = pl.BlockSpec(memory_space=pltpu.HBM)
    dma = pltpu.SemaphoreType.DMA
    out = pl.pallas_call(
        functools.partial(kernel, (tms, rws, fd, rd, cols, ch)),
        out_shape=jax.ShapeDtypeStruct((pix * ch // 128, 128), F32),
        in_specs=[pl.BlockSpec(memory_space=pltpu.SMEM), *[hbm] * 5],
        out_specs=vmem,
        scratch_shapes=[
            pltpu.VMEM(conv_two.shape, BF16),
            pltpu.VMEM(conv_one.shape, BF16),
            *[pltpu.VMEM((local, ch), BF16)] * 3,
            pltpu.VMEM((ch // 128, local, 128), F32),
            pltpu.VMEM((cols + 2, fd * rd, ch), BF16),
            *[pltpu.VMEM((cols, fd * rd, ch), BF16)] * 2,
            *[pltpu.VMEM((group, fd * rd, ch), BF16)] * 4,
            pltpu.VMEM((3, pix + 2 * rows, ch), BF16),
            pltpu.VMEM((3, pix + 2 * rows, ch), BF16),
            pltpu.VMEM((pix, 3 * ch), F32),
            pltpu.VMEM((pix, ch), F32),
            pltpu.VMEM((pix, ch), F32),
            dma((3,)),
            dma((2, 3)),
            *[dma] * 4,
            *[dma((2,))] * 2,
            *[dma] * 2,
            dma((2,)),
            dma((2, 4)),
        ],
        compiler_params=pltpu.CompilerParams(
            collective_id=0, has_side_effects=True, vmem_limit_bytes=50 * 1024 * 1024
        ),
        name="column_block",
    )(lengths, flat(cotangent), flat(hidden), flat(latents), in_hbm(conv_two), in_hbm(conv_one))
    return out.reshape(1, frames, rows, 1, ch)


def solution(mesh):
    in_specs = (
        P("dp", "tm", "rows", None, None),
        P("dp", "tm", "rows", None, None),
        P("dp", "tm", "rows", None, None),
        P(),
        P(),
        P("dp"),
    )
    out_specs = P("dp", None, None, ("tm", "rows"), None)
    return jax.shard_map(
        functools.partial(on_device, mesh.shape["tm"], mesh.shape["rows"]),
        mesh=mesh,
        in_specs=in_specs,
        out_specs=out_specs,
        check_vma=False,
    )
```

```python
import functools

import jax
import jax.numpy as jnp
from jax import lax
from jax.experimental import pallas as pl
from jax.experimental.pallas import tpu as pltpu
from jax.sharding import PartitionSpec as P

MESH = pl.DeviceIdType.MESH
NT = (((1,), (1,)), ((), ()))
F32 = jnp.float32
BF16 = jnp.bfloat16
SPLIT = 256


def silu_slope(values):
    gate = 1.0 / (1.0 + jnp.exp(-values))
    return gate * (1.0 + values * (1.0 - gate))


def kernel(
    sizes,
    len_ref,
    cot_ref,
    hid_ref,
    lat_ref,
    w_two,
    w_one,
    out_ref,
    wv_two,
    wv_one,
    cot_in,
    hid_in,
    lat_in,
    tmp,
    stage_c,
    stage_h,
    stage_l,
    recv_c,
    recv_o,
    recv_h,
    recv_l,
    cots,
    grads,
    acc,
    partial,
    slope_l,
    in_sem,
    w_sem,
    c_send,
    c_recv,
    o_send,
    o_recv,
    h_send,
    h_recv,
    l_send,
    l_recv,
    x_sem,
    g_sem,
):
    tms, rws, fd, rd, cols, ch = sizes
    group = tms * rws
    frames = tms * fd
    rows = rws * rd
    pix = frames * rows
    dp = lax.axis_index("dp")
    tm = lax.axis_index("tm")
    rw = lax.axis_index("rows")
    me = tm * rws + rw
    odd = lax.rem(rw, 2)
    mate_slot = 2 * odd
    outer_slot = 2 - 2 * odd

    chip = rw - odd
    chips = rws // 2

    def each_peer(action):
        for step in sorted(range(chips), key=lambda s: -min(s, chips - s)):

            def one(k, carry, step=step):
                if step == 0:
                    action(lax.rem(tm + k // 2, tms), chip + lax.rem(odd + k, 2))
                else:
                    action(
                        lax.rem(tm + k // 2 + tms // 2, tms), lax.rem(chip + 2 * step + lax.rem(k, 2), rws)
                    )
                return carry

            lax.fori_loop(1 if step == 0 else 0, 2 * tms, one, 0)

    own_copies = []
    for n, (src, dst) in enumerate(((cot_ref, cot_in), (hid_ref, hid_in), (lat_ref, lat_in))):
        own_copies.append(pltpu.make_async_copy(src, dst, in_sem.at[n]))
    own_copies[0].start()

    barrier = pltpu.get_barrier_semaphore()
    each_peer(
        lambda d_tm, d_rw: pl.semaphore_signal(
            barrier, inc=1, device_id=(dp, d_tm, d_rw), device_id_type=MESH
        )
    )

    own_copies[1].start()
    own_copies[2].start()
    weight_copies = []
    for n, (src, dst) in enumerate(((w_two, wv_two), (w_one, wv_one))):
        for at, c in enumerate((1, 0, 2)):
            copy = pltpu.make_async_copy(src.at[:, :, c], dst.at[:, :, c], w_sem.at[n, at])
            copy.start()
            weight_copies.append(copy)

    lanes = out_ref.shape[1]
    strips = ch // lanes
    row_of = lax.broadcasted_iota(jnp.int32, (fd * rd, lanes), 0)
    live = tm * fd + row_of // rd < len_ref[0]

    def columns_of(src_ref, dst_ref, first, masked):
        for j in range(strips):
            tmp[j] = src_ref[:, j * lanes : (j + 1) * lanes].astype(F32)

        def one(w, carry):
            for j in range(strips):
                block = tmp.at[j][pl.ds(w, fd * rd, stride=cols), :]
                if masked:
                    block = jnp.where(live, block, 0.0)
                dst_ref[first + w, :, j * lanes : (j + 1) * lanes] = block.astype(BF16)
            return carry

        lax.fori_loop(0, cols, one, 0)

    def outer_at(device):
        return device + 2 * lax.rem(device, 2)

    def send_all(stage, recv, at, send_sem, recv_sem, chans=None):
        chans = pl.ds(0, ch) if chans is None else chans

        each_peer(
            lambda d_tm, d_rw: pltpu.make_async_remote_copy(
                src_ref=stage.at[at(d_tm * rws + d_rw), :, chans],
                dst_ref=recv.at[me, :, chans],
                send_sem=send_sem,
                recv_sem=recv_sem,
                device_id=(dp, d_tm, d_rw),
                device_id_type=MESH,
            ).start()
        )

    def wait_all(recv, sem, chans=None):
        part = recv.at[pl.ds(0, group - 1), :, pl.ds(0, ch) if chans is None else chans]
        pltpu.make_async_copy(part, part, sem).wait()

    no_column = jnp.zeros((fd * rd, ch), BF16)
    stage_c[0] = no_column
    stage_c[cols + 1] = no_column
    blocks = (pl.ds(0, SPLIT), pl.ds(SPLIT, ch - SPLIT))
    own_copies[0].wait()
    columns_of(cot_in, stage_c, 1, True)
    pl.semaphore_wait(barrier, group - 1)
    send_all(stage_c, recv_c, lambda device: device + 1, c_send, c_recv)
    send_all(stage_c, recv_o, outer_at, o_send, o_recv)
    own_copies[1].wait()
    columns_of(hid_in, stage_h, 0, False)
    for at, chans in enumerate(blocks):
        send_all(stage_h, recv_h, lambda device: device, h_send.at[at], h_recv.at[at], chans)
    own_copies[2].wait()
    columns_of(lat_in, stage_l, 0, False)
    send_all(stage_l, recv_l, lambda device: device, l_send, l_recv)
    recv_c[me] = stage_c[me + 1]
    recv_o[me] = stage_c[outer_at(me)]
    recv_h[me] = stage_h[me]
    recv_l[me] = stage_l[me]

    tail = cots.shape[1] - pix
    for buf in (cots, grads):
        buf[:, pl.ds(pix, tail), :] = jnp.zeros((3, tail, ch), BF16)

    @pl.when((me == 0) | (me == group - 1))
    def _():
        grads[outer_slot, pl.ds(0, pix), :] = jnp.zeros((pix, ch), BF16)

    def gather_rows(recv, write, chans=slice(None)):
        for t in range(tms):
            for f in range(fd):
                for first in range(0, rws, 4):
                    parts = [recv[t * rws + first + i, f * rd : (f + 1) * rd, chans] for i in range(4)]
                    write(pl.ds((t * fd + f) * rows + first * rd, 4 * rd), chans, jnp.concatenate(parts, axis=0))

    def into(buf, slot):
        def write(at, chans, block):
            buf[slot, at, chans] = block

        return write

    def scaled_into(buf):
        def write(at, chans, block):
            buf[1, at, chans] = (partial[at, chans] * silu_slope(block.astype(F32))).astype(BF16)

        return write

    def slope_into(buf):
        def write(at, chans, block):
            buf[at, chans] = silu_slope(block.astype(F32))

        return write

    def copy_column(buf, chans, slot, target, send_sem, recv_sem):
        return pltpu.make_async_remote_copy(
            src_ref=buf.at[1, pl.ds(0, pix), chans],
            dst_ref=buf.at[slot, pl.ds(0, pix), chans],
            send_sem=send_sem,
            recv_sem=recv_sem,
            device_id=(dp, target // rws, lax.rem(target, rws)),
            device_id_type=MESH,
        )

    def to_mate(buf, chans, sems):
        return copy_column(buf, chans, outer_slot, me + 1 - 2 * odd, *sems)

    inner = (me > 0) & (me < group - 1)

    def to_outer(buf, chans, sems):
        return copy_column(buf, chans, mate_slot, lax.rem(me + 2 * odd - 1 + group, group), *sems)

    wait_all(recv_c, c_recv)
    gather_rows(recv_c, into(cots, 1))
    mate_copy = to_mate(cots, pl.ds(0, ch), (x_sem.at[0], x_sem.at[1]))
    mate_copy.start()

    def stacked(buf, columns, ins):
        parts = [buf[c, (2 - a) * rows : (2 - a) * rows + pix, ins] for c in columns for a in range(3)]
        return jnp.concatenate(parts, axis=1)

    def weights(wv, columns, outs, ins):
        return jnp.concatenate(
            [
                jnp.concatenate([wv[a, r, c, outs, ins] for c in columns for a in range(3)], axis=1)
                for r in range(3)
            ],
            axis=0,
        )

    def product(buf, wv, columns, outs, ins):
        return lax.dot_general(
            stacked(buf, columns, ins), weights(wv, columns, outs, ins), NT, preferred_element_type=F32
        )

    every = slice(0, ch)

    def row_taps(above, same, below):
        at_row = lax.rem(lax.broadcasted_iota(jnp.int32, above.shape, 0), rows)
        up = jnp.where(at_row == rows - 1, 0.0, pltpu.roll(above, pix - 1, 0))
        down = jnp.where(at_row == 0, 0.0, pltpu.roll(below, 1, 0))
        return same + up + down

    def shifted_product(buf, wv, column, ins):
        block = buf[column, :, ins].astype(F32)
        size = block.shape[0]
        at_row = lax.rem(lax.broadcasted_iota(jnp.int32, block.shape, 0), rows)
        above = jnp.where(at_row == rows - 1, 0.0, pltpu.roll(block, size - 1, 0))
        below = jnp.where(at_row == 0, 0.0, pltpu.roll(block, 1, 0))
        taps = [tap.astype(BF16) for tap in (above, block, below)]
        left = [taps[r][(2 - a) * rows : (2 - a) * rows + pix] for r in range(3) for a in range(3)]
        right = [wv[a, r, column, :, ins] for r in range(3) for a in range(3)]
        return lax.dot_general(
            jnp.concatenate(left, axis=1), jnp.concatenate(right, axis=1), NT, preferred_element_type=F32
        )

    weight_copies[0].wait()
    acc[...] = product(cots, wv_two, (1,), every, every)
    wait_all(recv_o, o_recv)
    gather_rows(recv_o, into(cots, outer_slot))
    for copy in weight_copies[1:3]:
        copy.wait()
    mate_copy.wait_recv()
    g_copies = []
    for at, outs in enumerate((slice(0, SPLIT), slice(SPLIT, ch))):
        n = outs.stop - outs.start
        part = product(cots, wv_two, (mate_slot, outer_slot), outs, every)
        taps = [acc[:, r * ch + outs.start : r * ch + outs.stop] + part[:, r * n : (r + 1) * n] for r in range(3)]
        partial[:, outs] = row_taps(*taps)
        wait_all(recv_h, h_recv.at[at], blocks[at])
        gather_rows(recv_h, slope_into(slope_l), outs)
        grads[1, pl.ds(0, pix), outs] = (partial[:, outs] * slope_l[:, outs]).astype(BF16)
        chans = pl.ds(outs.start, n)
        outer = to_outer(grads, chans, (g_sem.at[at, 0], g_sem.at[at, 1]))
        mate = to_mate(grads, chans, (g_sem.at[at, 2], g_sem.at[at, 3]))
        pl.when(inner)(outer.start)
        mate.start()
        g_copies.append((outer, mate))

    for copy in weight_copies[3:]:
        copy.wait()
    acc[...] = product(grads, wv_one, (1,), every, every)
    for _, mate in g_copies:
        mate.wait_recv()
    wait_all(recv_l, l_recv)
    gather_rows(recv_l, slope_into(slope_l))
    acc[...] += product(grads, wv_one, (mate_slot,), every, every)
    pl.when(inner)(g_copies[0][0].wait_recv)
    acc[...] += product(grads, wv_one, (outer_slot,), every, slice(0, SPLIT))
    pl.when(inner)(g_copies[1][0].wait_recv)
    part = product(grads, wv_one, (outer_slot,), every, slice(SPLIT, ch))
    taps = [acc[:, r * ch : (r + 1) * ch] + part[:, r * ch : (r + 1) * ch] for r in range(3)]
    result = cots[1, pl.ds(0, pix), :].astype(F32) + row_taps(*taps) * slope_l[...]
    for j in range(strips):
        out_ref[pl.ds(j, pix, stride=strips), :] = result[:, j * lanes : (j + 1) * lanes]

    wait_all(recv_c, c_send)
    wait_all(recv_o, o_send)
    for at, chans in enumerate(blocks):
        wait_all(recv_h, h_send.at[at], chans)
    wait_all(recv_l, l_send)
    mate_copy.wait_send()
    for outer, mate in g_copies:
        pl.when(inner)(outer.wait_send)
        mate.wait_send()


def on_device(tms, rws, latents, hidden, cotangent, conv_one, conv_two, lengths):
    _, fd, rd, cols, ch = latents.shape
    frames, rows = tms * fd, rws * rd
    pix = frames * rows
    local = fd * rd * cols
    group = tms * rws
    in_hbm = lambda x: pltpu.with_memory_space_constraint(x, pltpu.HBM)
    flat = lambda x: in_hbm(x.reshape(local, ch))
    vmem = pl.BlockSpec(memory_space=pltpu.VMEM)
    hbm = pl.BlockSpec(memory_space=pltpu.HBM)
    dma = pltpu.SemaphoreType.DMA
    out = pl.pallas_call(
        functools.partial(kernel, (tms, rws, fd, rd, cols, ch)),
        out_shape=jax.ShapeDtypeStruct((pix * ch // 128, 128), F32),
        in_specs=[pl.BlockSpec(memory_space=pltpu.SMEM), *[hbm] * 5],
        out_specs=vmem,
        scratch_shapes=[
            pltpu.VMEM(conv_two.shape, BF16),
            pltpu.VMEM(conv_one.shape, BF16),
            *[pltpu.VMEM((local, ch), BF16)] * 3,
            pltpu.VMEM((ch // 128, local, 128), F32),
            pltpu.VMEM((cols + 2, fd * rd, ch), BF16),
            *[pltpu.VMEM((cols, fd * rd, ch), BF16)] * 2,
            *[pltpu.VMEM((group, fd * rd, ch), BF16)] * 4,
            pltpu.VMEM((3, pix + 2 * rows, ch), BF16),
            pltpu.VMEM((3, pix + 2 * rows, ch), BF16),
            pltpu.VMEM((pix, 3 * ch), F32),
            pltpu.VMEM((pix, ch), F32),
            pltpu.VMEM((pix, ch), F32),
            dma((3,)),
            dma((2, 3)),
            *[dma] * 4,
            *[dma((2,))] * 2,
            *[dma] * 2,
            dma((2,)),
            dma((2, 4)),
        ],
        compiler_params=pltpu.CompilerParams(
            collective_id=0, has_side_effects=True, vmem_limit_bytes=50 * 1024 * 1024
        ),
        name="column_block",
    )(lengths, flat(cotangent), flat(hidden), flat(latents), in_hbm(conv_two), in_hbm(conv_one))
    return out.reshape(1, frames, rows, 1, ch)


def solution(mesh):
    in_specs = (
        P("dp", "tm", "rows", None, None),
        P("dp", "tm", "rows", None, None),
        P("dp", "tm", "rows", None, None),
        P(),
        P(),
        P("dp"),
    )
    out_specs = P("dp", None, None, ("tm", "rows"), None)
    return jax.shard_map(
        functools.partial(on_device, mesh.shape["tm"], mesh.shape["rows"]),
        mesh=mesh,
        in_specs=in_specs,
        out_specs=out_specs,
        check_vma=False,
    )
```

```python
import functools

import jax
import jax.numpy as jnp
from jax import lax
from jax.experimental import pallas as pl
from jax.experimental.pallas import tpu as pltpu
from jax.sharding import PartitionSpec as P

MESH = pl.DeviceIdType.MESH
NT = (((1,), (1,)), ((), ()))
F32 = jnp.float32
BF16 = jnp.bfloat16
SPLIT = 256


def silu_slope(values):
    gate = 1.0 / (1.0 + jnp.exp(-values))
    return gate * (1.0 + values * (1.0 - gate))


def kernel(
    sizes,
    len_ref,
    cot_ref,
    hid_ref,
    lat_ref,
    w_two,
    w_one,
    out_ref,
    wv_two,
    wv_one,
    cot_in,
    hid_in,
    lat_in,
    tmp,
    stage_c,
    stage_h,
    stage_l,
    recv_c,
    recv_o,
    recv_h,
    recv_l,
    cots,
    grads,
    acc,
    partial,
    slope_l,
    in_sem,
    w_sem,
    c_send,
    c_recv,
    o_send,
    o_recv,
    h_send,
    h_recv,
    l_send,
    l_recv,
    x_sem,
    g_sem,
):
    tms, rws, fd, rd, cols, ch = sizes
    group = tms * rws
    frames = tms * fd
    rows = rws * rd
    pix = frames * rows
    dp = lax.axis_index("dp")
    tm = lax.axis_index("tm")
    rw = lax.axis_index("rows")
    me = tm * rws + rw
    odd = lax.rem(rw, 2)
    mate_slot = 2 * odd
    outer_slot = 2 - 2 * odd

    chip = rw - odd
    chips = rws // 2

    def each_peer(action):
        for step in sorted(range(chips), key=lambda s: -min(s, chips - s)):

            def one(k, carry, step=step):
                if step == 0:
                    action(lax.rem(tm + k // 2, tms), chip + lax.rem(odd + k, 2))
                else:
                    action(
                        lax.rem(tm + k // 2 + tms // 2, tms), lax.rem(chip + 2 * step + lax.rem(k, 2), rws)
                    )
                return carry

            lax.fori_loop(1 if step == 0 else 0, 2 * tms, one, 0)

    own_copies = []
    for n, (src, dst) in enumerate(((cot_ref, cot_in), (hid_ref, hid_in), (lat_ref, lat_in))):
        own_copies.append(pltpu.make_async_copy(src, dst, in_sem.at[n]))
    own_copies[0].start()

    barrier = pltpu.get_barrier_semaphore()
    each_peer(
        lambda d_tm, d_rw: pl.semaphore_signal(
            barrier, inc=1, device_id=(dp, d_tm, d_rw), device_id_type=MESH
        )
    )

    own_copies[1].start()
    own_copies[2].start()
    weight_copies = []
    for n, (src, dst) in enumerate(((w_two, wv_two), (w_one, wv_one))):
        for at, c in enumerate((1, 0, 2)):
            copy = pltpu.make_async_copy(src.at[:, :, c], dst.at[:, :, c], w_sem.at[n, at])
            copy.start()
            weight_copies.append(copy)

    lanes = out_ref.shape[1]
    strips = ch // lanes
    row_of = lax.broadcasted_iota(jnp.int32, (fd * rd, lanes), 0)
    live = tm * fd + row_of // rd < len_ref[0]

    def columns_of(src_ref, dst_ref, first, masked):
        for j in range(strips):
            tmp[j] = src_ref[:, j * lanes : (j + 1) * lanes].astype(F32)

        def one(w, carry):
            for j in range(strips):
                block = tmp.at[j][pl.ds(w, fd * rd, stride=cols), :]
                if masked:
                    block = jnp.where(live, block, 0.0)
                dst_ref[first + w, :, j * lanes : (j + 1) * lanes] = block.astype(BF16)
            return carry

        lax.fori_loop(0, cols, one, 0)

    def outer_at(device):
        return device + 2 * lax.rem(device, 2)

    def send_all(stage, recv, at, send_sem, recv_sem, chans=None):
        chans = pl.ds(0, ch) if chans is None else chans

        each_peer(
            lambda d_tm, d_rw: pltpu.make_async_remote_copy(
                src_ref=stage.at[at(d_tm * rws + d_rw), :, chans],
                dst_ref=recv.at[me, :, chans],
                send_sem=send_sem,
                recv_sem=recv_sem,
                device_id=(dp, d_tm, d_rw),
                device_id_type=MESH,
            ).start()
        )

    def wait_all(recv, sem, chans=None):
        part = recv.at[pl.ds(0, group - 1), :, pl.ds(0, ch) if chans is None else chans]
        pltpu.make_async_copy(part, part, sem).wait()

    no_column = jnp.zeros((fd * rd, ch), BF16)
    stage_c[0] = no_column
    stage_c[cols + 1] = no_column
    blocks = (pl.ds(0, SPLIT), pl.ds(SPLIT, ch - SPLIT))
    own_copies[0].wait()
    columns_of(cot_in, stage_c, 1, True)
    pl.semaphore_wait(barrier, group - 1)
    send_all(stage_c, recv_c, lambda device: device + 1, c_send, c_recv)
    send_all(stage_c, recv_o, outer_at, o_send, o_recv)
    own_copies[1].wait()
    columns_of(hid_in, stage_h, 0, False)
    for at, chans in enumerate(blocks):
        send_all(stage_h, recv_h, lambda device: device, h_send.at[at], h_recv.at[at], chans)
    own_copies[2].wait()
    columns_of(lat_in, stage_l, 0, False)
    send_all(stage_l, recv_l, lambda device: device, l_send, l_recv)
    recv_c[me] = stage_c[me + 1]
    recv_o[me] = stage_c[outer_at(me)]
    recv_h[me] = stage_h[me]
    recv_l[me] = stage_l[me]

    tail = cots.shape[1] - pix
    for buf in (cots, grads):
        buf[:, pl.ds(pix, tail), :] = jnp.zeros((3, tail, ch), BF16)

    @pl.when((me == 0) | (me == group - 1))
    def _():
        grads[outer_slot, pl.ds(0, pix), :] = jnp.zeros((pix, ch), BF16)

    def gather_rows(recv, write, chans=slice(None)):
        for t in range(tms):
            for f in range(fd):
                for first in range(0, rws, 4):
                    parts = [recv[t * rws + first + i, f * rd : (f + 1) * rd, chans] for i in range(4)]
                    write(pl.ds((t * fd + f) * rows + first * rd, 4 * rd), chans, jnp.concatenate(parts, axis=0))

    def into(buf, slot):
        def write(at, chans, block):
            buf[slot, at, chans] = block

        return write

    def scaled_into(buf):
        def write(at, chans, block):
            buf[1, at, chans] = (partial[at, chans] * silu_slope(block.astype(F32))).astype(BF16)

        return write

    def slope_into(buf):
        def write(at, chans, block):
            buf[at, chans] = silu_slope(block.astype(F32))

        return write

    def copy_column(buf, chans, slot, target, send_sem, recv_sem):
        return pltpu.make_async_remote_copy(
            src_ref=buf.at[1, pl.ds(0, pix), chans],
            dst_ref=buf.at[slot, pl.ds(0, pix), chans],
            send_sem=send_sem,
            recv_sem=recv_sem,
            device_id=(dp, target // rws, lax.rem(target, rws)),
            device_id_type=MESH,
        )

    def to_mate(buf, chans, sems):
        return copy_column(buf, chans, outer_slot, me + 1 - 2 * odd, *sems)

    inner = (me > 0) & (me < group - 1)

    def to_outer(buf, chans, sems):
        return copy_column(buf, chans, mate_slot, lax.rem(me + 2 * odd - 1 + group, group), *sems)

    wait_all(recv_c, c_recv)
    gather_rows(recv_c, into(cots, 1))
    mate_copy = to_mate(cots, pl.ds(0, ch), (x_sem.at[0], x_sem.at[1]))
    mate_copy.start()

    def stacked(buf, columns, ins):
        parts = [buf[c, (2 - a) * rows : (2 - a) * rows + pix, ins] for c in columns for a in range(3)]
        return jnp.concatenate(parts, axis=1)

    def weights(wv, columns, outs, ins):
        return jnp.concatenate(
            [
                jnp.concatenate([wv[a, r, c, outs, ins] for c in columns for a in range(3)], axis=1)
                for r in range(3)
            ],
            axis=0,
        )

    def product(buf, wv, columns, outs, ins):
        return lax.dot_general(
            stacked(buf, columns, ins), weights(wv, columns, outs, ins), NT, preferred_element_type=F32
        )

    every = slice(0, ch)

    def row_taps(above, same, below):
        at_row = lax.rem(lax.broadcasted_iota(jnp.int32, above.shape, 0), rows)
        up = jnp.where(at_row == rows - 1, 0.0, pltpu.roll(above, pix - 1, 0))
        down = jnp.where(at_row == 0, 0.0, pltpu.roll(below, 1, 0))
        return same + up + down

    def shifted_product(buf, wv, column, ins):
        block = buf[column, :, ins].astype(F32)
        size = block.shape[0]
        at_row = lax.rem(lax.broadcasted_iota(jnp.int32, block.shape, 0), rows)
        above = jnp.where(at_row == rows - 1, 0.0, pltpu.roll(block, size - 1, 0))
        below = jnp.where(at_row == 0, 0.0, pltpu.roll(block, 1, 0))
        taps = [tap.astype(BF16) for tap in (above, block, below)]
        left = [taps[r][(2 - a) * rows : (2 - a) * rows + pix] for r in range(3) for a in range(3)]
        right = [wv[a, r, column, :, ins] for r in range(3) for a in range(3)]
        return lax.dot_general(
            jnp.concatenate(left, axis=1), jnp.concatenate(right, axis=1), NT, preferred_element_type=F32
        )

    weight_copies[0].wait()
    acc[...] = product(cots, wv_two, (1,), every, every)
    for copy in weight_copies[1:3]:
        copy.wait()
    mate_copy.wait_recv()
    early = product(cots, wv_two, (mate_slot,), slice(0, SPLIT), every)
    for r in range(3):
        acc[:, r * ch : r * ch + SPLIT] += early[:, r * SPLIT : (r + 1) * SPLIT]
    wait_all(recv_o, o_recv)
    gather_rows(recv_o, into(cots, outer_slot))
    g_copies = []
    for at, outs in enumerate((slice(0, SPLIT), slice(SPLIT, ch))):
        n = outs.stop - outs.start
        part = product(cots, wv_two, (outer_slot,) if at == 0 else (mate_slot, outer_slot), outs, every)
        taps = [acc[:, r * ch + outs.start : r * ch + outs.stop] + part[:, r * n : (r + 1) * n] for r in range(3)]
        partial[:, outs] = row_taps(*taps)
        wait_all(recv_h, h_recv.at[at], blocks[at])
        gather_rows(recv_h, slope_into(slope_l), outs)
        grads[1, pl.ds(0, pix), outs] = (partial[:, outs] * slope_l[:, outs]).astype(BF16)
        chans = pl.ds(outs.start, n)
        outer = to_outer(grads, chans, (g_sem.at[at, 0], g_sem.at[at, 1]))
        mate = to_mate(grads, chans, (g_sem.at[at, 2], g_sem.at[at, 3]))
        pl.when(inner)(outer.start)
        mate.start()
        g_copies.append((outer, mate))

    for copy in weight_copies[3:]:
        copy.wait()
    acc[...] = product(grads, wv_one, (1,), every, every)
    for _, mate in g_copies:
        mate.wait_recv()
    wait_all(recv_l, l_recv)
    gather_rows(recv_l, slope_into(slope_l))
    acc[...] += product(grads, wv_one, (mate_slot,), every, every)
    pl.when(inner)(g_copies[0][0].wait_recv)
    acc[...] += product(grads, wv_one, (outer_slot,), every, slice(0, SPLIT))
    pl.when(inner)(g_copies[1][0].wait_recv)
    part = product(grads, wv_one, (outer_slot,), every, slice(SPLIT, ch))
    taps = [acc[:, r * ch : (r + 1) * ch] + part[:, r * ch : (r + 1) * ch] for r in range(3)]
    result = cots[1, pl.ds(0, pix), :].astype(F32) + row_taps(*taps) * slope_l[...]
    for j in range(strips):
        out_ref[pl.ds(j, pix, stride=strips), :] = result[:, j * lanes : (j + 1) * lanes]

    wait_all(recv_c, c_send)
    wait_all(recv_o, o_send)
    for at, chans in enumerate(blocks):
        wait_all(recv_h, h_send.at[at], chans)
    wait_all(recv_l, l_send)
    mate_copy.wait_send()
    for outer, mate in g_copies:
        pl.when(inner)(outer.wait_send)
        mate.wait_send()


def on_device(tms, rws, latents, hidden, cotangent, conv_one, conv_two, lengths):
    _, fd, rd, cols, ch = latents.shape
    frames, rows = tms * fd, rws * rd
    pix = frames * rows
    local = fd * rd * cols
    group = tms * rws
    in_hbm = lambda x: pltpu.with_memory_space_constraint(x, pltpu.HBM)
    flat = lambda x: in_hbm(x.reshape(local, ch))
    vmem = pl.BlockSpec(memory_space=pltpu.VMEM)
    hbm = pl.BlockSpec(memory_space=pltpu.HBM)
    dma = pltpu.SemaphoreType.DMA
    out = pl.pallas_call(
        functools.partial(kernel, (tms, rws, fd, rd, cols, ch)),
        out_shape=jax.ShapeDtypeStruct((pix * ch // 128, 128), F32),
        in_specs=[pl.BlockSpec(memory_space=pltpu.SMEM), *[hbm] * 5],
        out_specs=vmem,
        scratch_shapes=[
            pltpu.VMEM(conv_two.shape, BF16),
            pltpu.VMEM(conv_one.shape, BF16),
            *[pltpu.VMEM((local, ch), BF16)] * 3,
            pltpu.VMEM((ch // 128, local, 128), F32),
            pltpu.VMEM((cols + 2, fd * rd, ch), BF16),
            *[pltpu.VMEM((cols, fd * rd, ch), BF16)] * 2,
            *[pltpu.VMEM((group, fd * rd, ch), BF16)] * 4,
            pltpu.VMEM((3, pix + 2 * rows, ch), BF16),
            pltpu.VMEM((3, pix + 2 * rows, ch), BF16),
            pltpu.VMEM((pix, 3 * ch), F32),
            pltpu.VMEM((pix, ch), F32),
            pltpu.VMEM((pix, ch), F32),
            dma((3,)),
            dma((2, 3)),
            *[dma] * 4,
            *[dma((2,))] * 2,
            *[dma] * 2,
            dma((2,)),
            dma((2, 4)),
        ],
        compiler_params=pltpu.CompilerParams(
            collective_id=0, has_side_effects=True, vmem_limit_bytes=50 * 1024 * 1024
        ),
        name="column_block",
    )(lengths, flat(cotangent), flat(hidden), flat(latents), in_hbm(conv_two), in_hbm(conv_one))
    return out.reshape(1, frames, rows, 1, ch)


def solution(mesh):
    in_specs = (
        P("dp", "tm", "rows", None, None),
        P("dp", "tm", "rows", None, None),
        P("dp", "tm", "rows", None, None),
        P(),
        P(),
        P("dp"),
    )
    out_specs = P("dp", None, None, ("tm", "rows"), None)
    return jax.shard_map(
        functools.partial(on_device, mesh.shape["tm"], mesh.shape["rows"]),
        mesh=mesh,
        in_specs=in_specs,
        out_specs=out_specs,
        check_vma=False,
    )
```

```python
import functools

import jax
import jax.numpy as jnp
from jax import lax
from jax.experimental import pallas as pl
from jax.experimental.pallas import tpu as pltpu
from jax.sharding import PartitionSpec as P

MESH = pl.DeviceIdType.MESH
NT = (((1,), (1,)), ((), ()))
F32 = jnp.float32
BF16 = jnp.bfloat16
SPLIT = 256


def silu_slope(values):
    gate = 1.0 / (1.0 + jnp.exp(-values))
    return gate * (1.0 + values * (1.0 - gate))


def kernel(
    sizes,
    len_ref,
    cot_ref,
    hid_ref,
    lat_ref,
    w_two,
    w_one,
    out_ref,
    wv_two,
    wv_one,
    cot_in,
    hid_in,
    lat_in,
    tmp,
    stage_c,
    stage_h,
    stage_l,
    recv_c,
    recv_o,
    recv_h,
    recv_l,
    cots,
    grads,
    acc,
    partial,
    slope_l,
    in_sem,
    w_sem,
    c_send,
    c_recv,
    o_send,
    o_recv,
    h_send,
    h_recv,
    l_send,
    l_recv,
    x_sem,
    g_sem,
):
    tms, rws, fd, rd, cols, ch = sizes
    group = tms * rws
    frames = tms * fd
    rows = rws * rd
    pix = frames * rows
    dp = lax.axis_index("dp")
    tm = lax.axis_index("tm")
    rw = lax.axis_index("rows")
    me = tm * rws + rw
    odd = lax.rem(rw, 2)
    mate_slot = 2 * odd
    outer_slot = 2 - 2 * odd

    chip = rw - odd
    chips = rws // 2

    def each_peer(action):
        for step in sorted(range(chips), key=lambda s: -min(s, chips - s)):

            def one(k, carry, step=step):
                if step == 0:
                    action(lax.rem(tm + k // 2, tms), chip + lax.rem(odd + k, 2))
                else:
                    action(
                        lax.rem(tm + k // 2 + tms // 2, tms), lax.rem(chip + 2 * step + lax.rem(k, 2), rws)
                    )
                return carry

            lax.fori_loop(1 if step == 0 else 0, 2 * tms, one, 0)

    own_copies = []
    for n, (src, dst) in enumerate(((cot_ref, cot_in), (hid_ref, hid_in), (lat_ref, lat_in))):
        own_copies.append(pltpu.make_async_copy(src, dst, in_sem.at[n]))
    own_copies[0].start()

    barrier = pltpu.get_barrier_semaphore()
    each_peer(
        lambda d_tm, d_rw: pl.semaphore_signal(
            barrier, inc=1, device_id=(dp, d_tm, d_rw), device_id_type=MESH
        )
    )

    own_copies[1].start()
    own_copies[2].start()
    weight_copies = []
    for n, (src, dst) in enumerate(((w_two, wv_two), (w_one, wv_one))):
        for at, c in enumerate((1, 0, 2)):
            copy = pltpu.make_async_copy(src.at[:, :, c], dst.at[:, :, c], w_sem.at[n, at])
            copy.start()
            weight_copies.append(copy)

    lanes = out_ref.shape[1]
    strips = ch // lanes
    row_of = lax.broadcasted_iota(jnp.int32, (fd * rd, lanes), 0)
    live = tm * fd + row_of // rd < len_ref[0]

    def columns_of(src_ref, dst_ref, first, masked):
        for j in range(strips):
            tmp[j] = src_ref[:, j * lanes : (j + 1) * lanes].astype(F32)

        for w in range(cols):
            for j in range(strips):
                block = tmp.at[j][pl.ds(w, fd * rd, stride=cols), :]
                if masked:
                    block = jnp.where(live, block, 0.0)
                dst_ref[first + w, :, j * lanes : (j + 1) * lanes] = block.astype(BF16)

    def outer_at(device):
        return device + 2 * lax.rem(device, 2)

    def send_all(stage, recv, at, send_sem, recv_sem, chans=None):
        chans = pl.ds(0, ch) if chans is None else chans

        each_peer(
            lambda d_tm, d_rw: pltpu.make_async_remote_copy(
                src_ref=stage.at[at(d_tm * rws + d_rw), :, chans],
                dst_ref=recv.at[me, :, chans],
                send_sem=send_sem,
                recv_sem=recv_sem,
                device_id=(dp, d_tm, d_rw),
                device_id_type=MESH,
            ).start()
        )

    def wait_all(recv, sem, chans=None):
        part = recv.at[pl.ds(0, group - 1), :, pl.ds(0, ch) if chans is None else chans]
        pltpu.make_async_copy(part, part, sem).wait()

    no_column = jnp.zeros((fd * rd, ch), BF16)
    stage_c[0] = no_column
    stage_c[cols + 1] = no_column
    blocks = (pl.ds(0, SPLIT), pl.ds(SPLIT, ch - SPLIT))
    own_copies[0].wait()
    columns_of(cot_in, stage_c, 1, True)
    pl.semaphore_wait(barrier, group - 1)
    send_all(stage_c, recv_c, lambda device: device + 1, c_send, c_recv)
    send_all(stage_c, recv_o, outer_at, o_send, o_recv)
    own_copies[1].wait()
    columns_of(hid_in, stage_h, 0, False)
    for at, chans in enumerate(blocks):
        send_all(stage_h, recv_h, lambda device: device, h_send.at[at], h_recv.at[at], chans)
    own_copies[2].wait()
    columns_of(lat_in, stage_l, 0, False)
    send_all(stage_l, recv_l, lambda device: device, l_send, l_recv)
    recv_c[me] = stage_c[me + 1]
    recv_o[me] = stage_c[outer_at(me)]
    recv_h[me] = stage_h[me]
    recv_l[me] = stage_l[me]

    tail = cots.shape[1] - pix
    for buf in (cots, grads):
        buf[:, pl.ds(pix, tail), :] = jnp.zeros((3, tail, ch), BF16)

    @pl.when((me == 0) | (me == group - 1))
    def _():
        grads[outer_slot, pl.ds(0, pix), :] = jnp.zeros((pix, ch), BF16)

    def gather_rows(recv, write, chans=slice(None)):
        for t in range(tms):
            for f in range(fd):
                for first in range(0, rws, 4):
                    parts = [recv[t * rws + first + i, f * rd : (f + 1) * rd, chans] for i in range(4)]
                    write(pl.ds((t * fd + f) * rows + first * rd, 4 * rd), chans, jnp.concatenate(parts, axis=0))

    def into(buf, slot):
        def write(at, chans, block):
            buf[slot, at, chans] = block

        return write

    def scaled_into(buf):
        def write(at, chans, block):
            buf[1, at, chans] = (partial[at, chans] * silu_slope(block.astype(F32))).astype(BF16)

        return write

    def slope_into(buf):
        def write(at, chans, block):
            buf[at, chans] = silu_slope(block.astype(F32))

        return write

    def copy_column(buf, chans, slot, target, send_sem, recv_sem):
        return pltpu.make_async_remote_copy(
            src_ref=buf.at[1, pl.ds(0, pix), chans],
            dst_ref=buf.at[slot, pl.ds(0, pix), chans],
            send_sem=send_sem,
            recv_sem=recv_sem,
            device_id=(dp, target // rws, lax.rem(target, rws)),
            device_id_type=MESH,
        )

    def to_mate(buf, chans, sems):
        return copy_column(buf, chans, outer_slot, me + 1 - 2 * odd, *sems)

    inner = (me > 0) & (me < group - 1)

    def to_outer(buf, chans, sems):
        return copy_column(buf, chans, mate_slot, lax.rem(me + 2 * odd - 1 + group, group), *sems)

    wait_all(recv_c, c_recv)
    gather_rows(recv_c, into(cots, 1))
    mate_copy = to_mate(cots, pl.ds(0, ch), (x_sem.at[0], x_sem.at[1]))
    mate_copy.start()

    def stacked(buf, columns, ins):
        parts = [buf[c, (2 - a) * rows : (2 - a) * rows + pix, ins] for c in columns for a in range(3)]
        return jnp.concatenate(parts, axis=1)

    def weights(wv, columns, outs, ins):
        return jnp.concatenate(
            [
                jnp.concatenate([wv[a, r, c, outs, ins] for c in columns for a in range(3)], axis=1)
                for r in range(3)
            ],
            axis=0,
        )

    def product(buf, wv, columns, outs, ins):
        return lax.dot_general(
            stacked(buf, columns, ins), weights(wv, columns, outs, ins), NT, preferred_element_type=F32
        )

    every = slice(0, ch)

    def row_taps(above, same, below):
        at_row = lax.rem(lax.broadcasted_iota(jnp.int32, above.shape, 0), rows)
        up = jnp.where(at_row == rows - 1, 0.0, pltpu.roll(above, pix - 1, 0))
        down = jnp.where(at_row == 0, 0.0, pltpu.roll(below, 1, 0))
        return same + up + down

    def shifted_product(buf, wv, column, ins):
        block = buf[column, :, ins].astype(F32)
        size = block.shape[0]
        at_row = lax.rem(lax.broadcasted_iota(jnp.int32, block.shape, 0), rows)
        above = jnp.where(at_row == rows - 1, 0.0, pltpu.roll(block, size - 1, 0))
        below = jnp.where(at_row == 0, 0.0, pltpu.roll(block, 1, 0))
        taps = [tap.astype(BF16) for tap in (above, block, below)]
        left = [taps[r][(2 - a) * rows : (2 - a) * rows + pix] for r in range(3) for a in range(3)]
        right = [wv[a, r, column, :, ins] for r in range(3) for a in range(3)]
        return lax.dot_general(
            jnp.concatenate(left, axis=1), jnp.concatenate(right, axis=1), NT, preferred_element_type=F32
        )

    weight_copies[0].wait()
    acc[...] = product(cots, wv_two, (1,), every, every)
    for copy in weight_copies[1:3]:
        copy.wait()
    mate_copy.wait_recv()
    early = product(cots, wv_two, (mate_slot,), slice(0, SPLIT), every)
    for r in range(3):
        acc[:, r * ch : r * ch + SPLIT] += early[:, r * SPLIT : (r + 1) * SPLIT]
    wait_all(recv_o, o_recv)
    gather_rows(recv_o, into(cots, outer_slot))
    g_copies = []
    for at, outs in enumerate((slice(0, SPLIT), slice(SPLIT, ch))):
        n = outs.stop - outs.start
        part = product(cots, wv_two, (outer_slot,) if at == 0 else (mate_slot, outer_slot), outs, every)
        taps = [acc[:, r * ch + outs.start : r * ch + outs.stop] + part[:, r * n : (r + 1) * n] for r in range(3)]
        partial[:, outs] = row_taps(*taps)
        wait_all(recv_h, h_recv.at[at], blocks[at])
        gather_rows(recv_h, slope_into(slope_l), outs)
        grads[1, pl.ds(0, pix), outs] = (partial[:, outs] * slope_l[:, outs]).astype(BF16)
        chans = pl.ds(outs.start, n)
        outer = to_outer(grads, chans, (g_sem.at[at, 0], g_sem.at[at, 1]))
        mate = to_mate(grads, chans, (g_sem.at[at, 2], g_sem.at[at, 3]))
        pl.when(inner)(outer.start)
        mate.start()
        g_copies.append((outer, mate))

    for copy in weight_copies[3:]:
        copy.wait()
    acc[...] = product(grads, wv_one, (1,), every, every)
    for _, mate in g_copies:
        mate.wait_recv()
    wait_all(recv_l, l_recv)
    gather_rows(recv_l, slope_into(slope_l))
    acc[...] += product(grads, wv_one, (mate_slot,), every, every)
    pl.when(inner)(g_copies[0][0].wait_recv)
    acc[...] += product(grads, wv_one, (outer_slot,), every, slice(0, SPLIT))
    pl.when(inner)(g_copies[1][0].wait_recv)
    part = product(grads, wv_one, (outer_slot,), every, slice(SPLIT, ch))
    taps = [acc[:, r * ch : (r + 1) * ch] + part[:, r * ch : (r + 1) * ch] for r in range(3)]
    result = cots[1, pl.ds(0, pix), :].astype(F32) + row_taps(*taps) * slope_l[...]
    for j in range(strips):
        out_ref[pl.ds(j, pix, stride=strips), :] = result[:, j * lanes : (j + 1) * lanes]

    wait_all(recv_c, c_send)
    wait_all(recv_o, o_send)
    for at, chans in enumerate(blocks):
        wait_all(recv_h, h_send.at[at], chans)
    wait_all(recv_l, l_send)
    mate_copy.wait_send()
    for outer, mate in g_copies:
        pl.when(inner)(outer.wait_send)
        mate.wait_send()


def on_device(tms, rws, latents, hidden, cotangent, conv_one, conv_two, lengths):
    _, fd, rd, cols, ch = latents.shape
    frames, rows = tms * fd, rws * rd
    pix = frames * rows
    local = fd * rd * cols
    group = tms * rws
    in_hbm = lambda x: pltpu.with_memory_space_constraint(x, pltpu.HBM)
    flat = lambda x: in_hbm(x.reshape(local, ch))
    vmem = pl.BlockSpec(memory_space=pltpu.VMEM)
    hbm = pl.BlockSpec(memory_space=pltpu.HBM)
    dma = pltpu.SemaphoreType.DMA
    out = pl.pallas_call(
        functools.partial(kernel, (tms, rws, fd, rd, cols, ch)),
        out_shape=jax.ShapeDtypeStruct((pix * ch // 128, 128), F32),
        in_specs=[pl.BlockSpec(memory_space=pltpu.SMEM), *[hbm] * 5],
        out_specs=vmem,
        scratch_shapes=[
            pltpu.VMEM(conv_two.shape, BF16),
            pltpu.VMEM(conv_one.shape, BF16),
            *[pltpu.VMEM((local, ch), BF16)] * 3,
            pltpu.VMEM((ch // 128, local, 128), F32),
            pltpu.VMEM((cols + 2, fd * rd, ch), BF16),
            *[pltpu.VMEM((cols, fd * rd, ch), BF16)] * 2,
            *[pltpu.VMEM((group, fd * rd, ch), BF16)] * 4,
            pltpu.VMEM((3, pix + 2 * rows, ch), BF16),
            pltpu.VMEM((3, pix + 2 * rows, ch), BF16),
            pltpu.VMEM((pix, 3 * ch), F32),
            pltpu.VMEM((pix, ch), F32),
            pltpu.VMEM((pix, ch), F32),
            dma((3,)),
            dma((2, 3)),
            *[dma] * 4,
            *[dma((2,))] * 2,
            *[dma] * 2,
            dma((2,)),
            dma((2, 4)),
        ],
        compiler_params=pltpu.CompilerParams(
            collective_id=0, has_side_effects=True, vmem_limit_bytes=50 * 1024 * 1024
        ),
        name="column_block",
    )(lengths, flat(cotangent), flat(hidden), flat(latents), in_hbm(conv_two), in_hbm(conv_one))
    return out.reshape(1, frames, rows, 1, ch)


def solution(mesh):
    in_specs = (
        P("dp", "tm", "rows", None, None),
        P("dp", "tm", "rows", None, None),
        P("dp", "tm", "rows", None, None),
        P(),
        P(),
        P("dp"),
    )
    out_specs = P("dp", None, None, ("tm", "rows"), None)
    return jax.shard_map(
        functools.partial(on_device, mesh.shape["tm"], mesh.shape["rows"]),
        mesh=mesh,
        in_specs=in_specs,
        out_specs=out_specs,
        check_vma=False,
    )
```

```python
import functools

import jax
import jax.numpy as jnp
from jax import lax
from jax.experimental import pallas as pl
from jax.experimental.pallas import tpu as pltpu
from jax.sharding import PartitionSpec as P

MESH = pl.DeviceIdType.MESH
NT = (((1,), (1,)), ((), ()))
F32 = jnp.float32
BF16 = jnp.bfloat16
SPLIT = 256


def silu_slope(values):
    gate = 1.0 / (1.0 + jnp.exp(-values))
    return gate * (1.0 + values * (1.0 - gate))


def kernel(
    sizes,
    len_ref,
    cot_ref,
    hid_ref,
    lat_ref,
    w_two,
    w_one,
    out_ref,
    wv_two,
    wv_one,
    cot_in,
    hid_in,
    lat_in,
    tmp,
    stage_c,
    stage_h,
    stage_l,
    recv_c,
    recv_o,
    recv_h,
    recv_l,
    cots,
    grads,
    acc,
    partial,
    slope_l,
    in_sem,
    w_sem,
    c_send,
    c_recv,
    o_send,
    o_recv,
    h_send,
    h_recv,
    l_send,
    l_recv,
    x_sem,
    g_sem,
):
    tms, rws, fd, rd, cols, ch = sizes
    group = tms * rws
    frames = tms * fd
    rows = rws * rd
    pix = frames * rows
    dp = lax.axis_index("dp")
    tm = lax.axis_index("tm")
    rw = lax.axis_index("rows")
    me = tm * rws + rw
    odd = lax.rem(rw, 2)
    mate_slot = 2 * odd
    outer_slot = 2 - 2 * odd

    chip = rw - odd
    chips = rws // 2

    def each_peer(action):
        for step in sorted(range(chips), key=lambda s: -min(s, chips - s)):

            def one(k, carry, step=step):
                if step == 0:
                    action(lax.rem(tm + k // 2, tms), chip + lax.rem(odd + k, 2))
                else:
                    action(
                        lax.rem(tm + k // 2 + tms // 2, tms), lax.rem(chip + 2 * step + lax.rem(k, 2), rws)
                    )
                return carry

            lax.fori_loop(1 if step == 0 else 0, 2 * tms, one, 0)

    own_copies = []
    for n, (src, dst) in enumerate(((cot_ref, cot_in), (hid_ref, hid_in), (lat_ref, lat_in))):
        own_copies.append(pltpu.make_async_copy(src, dst, in_sem.at[n]))
    own_copies[0].start()

    barrier = pltpu.get_barrier_semaphore()
    each_peer(
        lambda d_tm, d_rw: pl.semaphore_signal(
            barrier, inc=1, device_id=(dp, d_tm, d_rw), device_id_type=MESH
        )
    )

    own_copies[1].start()
    own_copies[2].start()
    weight_copies = []
    for n, (src, dst) in enumerate(((w_two, wv_two), (w_one, wv_one))):
        for at, c in enumerate((1, 0, 2)):
            copy = pltpu.make_async_copy(src.at[:, :, c], dst.at[:, :, c], w_sem.at[n, at])
            copy.start()
            weight_copies.append(copy)

    lanes = out_ref.shape[1]
    strips = ch // lanes
    row_of = lax.broadcasted_iota(jnp.int32, (fd * rd, lanes), 0)
    live = tm * fd + row_of // rd < len_ref[0]

    def columns_of(src_ref, dst_ref, first, masked):
        for j in range(strips):
            tmp[j] = src_ref[:, j * lanes : (j + 1) * lanes].astype(F32)

        for w in range(cols):
            for j in range(strips):
                block = tmp.at[j][pl.ds(w, fd * rd, stride=cols), :]
                if masked:
                    block = jnp.where(live, block, 0.0)
                dst_ref[first + w, :, j * lanes : (j + 1) * lanes] = block.astype(BF16)

    def outer_at(device):
        return device + 2 * lax.rem(device, 2)

    def send_all(stage, recv, at, send_sem, recv_sem, chans=None):
        chans = pl.ds(0, ch) if chans is None else chans

        each_peer(
            lambda d_tm, d_rw: pltpu.make_async_remote_copy(
                src_ref=stage.at[at(d_tm * rws + d_rw), :, chans],
                dst_ref=recv.at[me, :, chans],
                send_sem=send_sem,
                recv_sem=recv_sem,
                device_id=(dp, d_tm, d_rw),
                device_id_type=MESH,
            ).start()
        )

    def wait_all(recv, sem, chans=None):
        part = recv.at[pl.ds(0, group - 1), :, pl.ds(0, ch) if chans is None else chans]
        pltpu.make_async_copy(part, part, sem).wait()

    no_column = jnp.zeros((fd * rd, ch), BF16)
    stage_c[0] = no_column
    stage_c[cols + 1] = no_column
    blocks = (pl.ds(0, SPLIT), pl.ds(SPLIT, ch - SPLIT))
    own_copies[0].wait()
    columns_of(cot_in, stage_c, 1, True)
    pl.semaphore_wait(barrier, group - 1)
    send_all(stage_c, recv_c, lambda device: device + 1, c_send, c_recv)
    send_all(stage_c, recv_o, outer_at, o_send, o_recv)
    own_copies[1].wait()
    columns_of(hid_in, stage_h, 0, False)
    for at, chans in enumerate(blocks):
        send_all(stage_h, recv_h, lambda device: device, h_send.at[at], h_recv.at[at], chans)
    own_copies[2].wait()
    columns_of(lat_in, stage_l, 0, False)
    send_all(stage_l, recv_l, lambda device: device, l_send, l_recv)
    recv_c[me] = stage_c[me + 1]
    recv_o[me] = stage_c[outer_at(me)]
    recv_h[me] = stage_h[me]
    recv_l[me] = stage_l[me]

    tail = cots.shape[1] - pix
    for buf in (cots, grads):
        buf[:, pl.ds(pix, tail), :] = jnp.zeros((3, tail, ch), BF16)

    @pl.when((me == 0) | (me == group - 1))
    def _():
        grads[outer_slot, pl.ds(0, pix), :] = jnp.zeros((pix, ch), BF16)

    def gather_rows(recv, write, chans=slice(None)):
        for t in range(tms):
            for f in range(fd):
                for first in range(0, rws, 4):
                    parts = [recv[t * rws + first + i, f * rd : (f + 1) * rd, chans] for i in range(4)]
                    write(pl.ds((t * fd + f) * rows + first * rd, 4 * rd), chans, jnp.concatenate(parts, axis=0))

    def into(buf, slot):
        def write(at, chans, block):
            buf[slot, at, chans] = block

        return write

    def scaled_into(buf):
        def write(at, chans, block):
            buf[1, at, chans] = (partial[at, chans] * silu_slope(block.astype(F32))).astype(BF16)

        return write

    def slope_into(buf):
        def write(at, chans, block):
            buf[at, chans] = silu_slope(block.astype(F32))

        return write

    def copy_column(buf, chans, slot, target, send_sem, recv_sem):
        return pltpu.make_async_remote_copy(
            src_ref=buf.at[1, pl.ds(0, pix), chans],
            dst_ref=buf.at[slot, pl.ds(0, pix), chans],
            send_sem=send_sem,
            recv_sem=recv_sem,
            device_id=(dp, target // rws, lax.rem(target, rws)),
            device_id_type=MESH,
        )

    def to_mate(buf, chans, sems):
        return copy_column(buf, chans, outer_slot, me + 1 - 2 * odd, *sems)

    inner = (me > 0) & (me < group - 1)

    def to_outer(buf, chans, sems):
        return copy_column(buf, chans, mate_slot, lax.rem(me + 2 * odd - 1 + group, group), *sems)

    wait_all(recv_c, c_recv)
    gather_rows(recv_c, into(cots, 1))
    mate_copy = to_mate(cots, pl.ds(0, ch), (x_sem.at[0], x_sem.at[1]))
    mate_copy.start()

    def stacked(buf, columns, ins):
        parts = [buf[c, (2 - a) * rows : (2 - a) * rows + pix, ins] for c in columns for a in range(3)]
        return jnp.concatenate(parts, axis=1)

    def weights(wv, columns, outs, ins):
        return jnp.concatenate(
            [
                jnp.concatenate([wv[a, r, c, outs, ins] for c in columns for a in range(3)], axis=1)
                for r in range(3)
            ],
            axis=0,
        )

    def product(buf, wv, columns, outs, ins):
        return lax.dot_general(
            stacked(buf, columns, ins), weights(wv, columns, outs, ins), NT, preferred_element_type=F32
        )

    every = slice(0, ch)

    def row_taps(above, same, below):
        at_row = lax.rem(lax.broadcasted_iota(jnp.int32, above.shape, 0), rows)
        up = jnp.where(at_row == rows - 1, 0.0, pltpu.roll(above, pix - 1, 0))
        down = jnp.where(at_row == 0, 0.0, pltpu.roll(below, 1, 0))
        return same + up + down

    def shifted_product(buf, wv, column, ins):
        block = buf[column, :, ins].astype(F32)
        size = block.shape[0]
        at_row = lax.rem(lax.broadcasted_iota(jnp.int32, block.shape, 0), rows)
        above = jnp.where(at_row == rows - 1, 0.0, pltpu.roll(block, size - 1, 0))
        below = jnp.where(at_row == 0, 0.0, pltpu.roll(block, 1, 0))
        taps = [tap.astype(BF16) for tap in (above, block, below)]
        left = [taps[r][(2 - a) * rows : (2 - a) * rows + pix] for r in range(3) for a in range(3)]
        right = [wv[a, r, column, :, ins] for r in range(3) for a in range(3)]
        return lax.dot_general(
            jnp.concatenate(left, axis=1), jnp.concatenate(right, axis=1), NT, preferred_element_type=F32
        )

    weight_copies[0].wait()
    acc[...] = product(cots, wv_two, (1,), every, every)
    for copy in weight_copies[1:3]:
        copy.wait()
    mate_copy.wait_recv()
    early = product(cots, wv_two, (mate_slot,), slice(0, SPLIT), every)
    for r in range(3):
        acc[:, r * ch : r * ch + SPLIT] += early[:, r * SPLIT : (r + 1) * SPLIT]
    wait_all(recv_o, o_recv)
    gather_rows(recv_o, into(cots, outer_slot))
    g_copies = []
    for at, outs in enumerate((slice(0, SPLIT), slice(SPLIT, ch))):
        n = outs.stop - outs.start
        part = product(cots, wv_two, (outer_slot,) if at == 0 else (mate_slot, outer_slot), outs, every)
        taps = [acc[:, r * ch + outs.start : r * ch + outs.stop] + part[:, r * n : (r + 1) * n] for r in range(3)]
        partial[:, outs] = row_taps(*taps)
        wait_all(recv_h, h_recv.at[at], blocks[at])
        gather_rows(recv_h, slope_into(slope_l), outs)
        grads[1, pl.ds(0, pix), outs] = (partial[:, outs] * slope_l[:, outs]).astype(BF16)
        chans = pl.ds(outs.start, n)
        outer = to_outer(grads, chans, (g_sem.at[at, 0], g_sem.at[at, 1]))
        mate = to_mate(grads, chans, (g_sem.at[at, 2], g_sem.at[at, 3]))
        pl.when(inner)(outer.start)
        mate.start()
        g_copies.append((outer, mate))

    for copy in weight_copies[3:]:
        copy.wait()
    acc[...] = product(grads, wv_one, (1,), every, every)
    for _, mate in g_copies:
        mate.wait_recv()
    wait_all(recv_l, l_recv)
    gather_rows(recv_l, slope_into(slope_l))
    acc[...] += product(grads, wv_one, (mate_slot,), every, every)
    wait_all(recv_c, c_send)
    wait_all(recv_o, o_send)
    for at, chans in enumerate(blocks):
        wait_all(recv_h, h_send.at[at], chans)
    wait_all(recv_l, l_send)
    mate_copy.wait_send()
    pl.when(inner)(g_copies[0][0].wait_recv)
    acc[...] += product(grads, wv_one, (outer_slot,), every, slice(0, SPLIT))
    pl.when(inner)(g_copies[1][0].wait_recv)
    part = product(grads, wv_one, (outer_slot,), every, slice(SPLIT, ch))
    taps = [acc[:, r * ch : (r + 1) * ch] + part[:, r * ch : (r + 1) * ch] for r in range(3)]
    result = cots[1, pl.ds(0, pix), :].astype(F32) + row_taps(*taps) * slope_l[...]
    for j in range(strips):
        out_ref[pl.ds(j, pix, stride=strips), :] = result[:, j * lanes : (j + 1) * lanes]

    for outer, mate in g_copies:
        pl.when(inner)(outer.wait_send)
        mate.wait_send()


def on_device(tms, rws, latents, hidden, cotangent, conv_one, conv_two, lengths):
    _, fd, rd, cols, ch = latents.shape
    frames, rows = tms * fd, rws * rd
    pix = frames * rows
    local = fd * rd * cols
    group = tms * rws
    in_hbm = lambda x: pltpu.with_memory_space_constraint(x, pltpu.HBM)
    flat = lambda x: in_hbm(x.reshape(local, ch))
    vmem = pl.BlockSpec(memory_space=pltpu.VMEM)
    hbm = pl.BlockSpec(memory_space=pltpu.HBM)
    dma = pltpu.SemaphoreType.DMA
    out = pl.pallas_call(
        functools.partial(kernel, (tms, rws, fd, rd, cols, ch)),
        out_shape=jax.ShapeDtypeStruct((pix * ch // 128, 128), F32),
        in_specs=[pl.BlockSpec(memory_space=pltpu.SMEM), *[hbm] * 5],
        out_specs=vmem,
        scratch_shapes=[
            pltpu.VMEM(conv_two.shape, BF16),
            pltpu.VMEM(conv_one.shape, BF16),
            *[pltpu.VMEM((local, ch), BF16)] * 3,
            pltpu.VMEM((ch // 128, local, 128), F32),
            pltpu.VMEM((cols + 2, fd * rd, ch), BF16),
            *[pltpu.VMEM((cols, fd * rd, ch), BF16)] * 2,
            *[pltpu.VMEM((group, fd * rd, ch), BF16)] * 4,
            pltpu.VMEM((3, pix + 2 * rows, ch), BF16),
            pltpu.VMEM((3, pix + 2 * rows, ch), BF16),
            pltpu.VMEM((pix, 3 * ch), F32),
            pltpu.VMEM((pix, ch), F32),
            pltpu.VMEM((pix, ch), F32),
            dma((3,)),
            dma((2, 3)),
            *[dma] * 4,
            *[dma((2,))] * 2,
            *[dma] * 2,
            dma((2,)),
            dma((2, 4)),
        ],
        compiler_params=pltpu.CompilerParams(
            collective_id=0, has_side_effects=True, vmem_limit_bytes=50 * 1024 * 1024
        ),
        name="column_block",
    )(lengths, flat(cotangent), flat(hidden), flat(latents), in_hbm(conv_two), in_hbm(conv_one))
    return out.reshape(1, frames, rows, 1, ch)


def solution(mesh):
    in_specs = (
        P("dp", "tm", "rows", None, None),
        P("dp", "tm", "rows", None, None),
        P("dp", "tm", "rows", None, None),
        P(),
        P(),
        P("dp"),
    )
    out_specs = P("dp", None, None, ("tm", "rows"), None)
    return jax.shard_map(
        functools.partial(on_device, mesh.shape["tm"], mesh.shape["rows"]),
        mesh=mesh,
        in_specs=in_specs,
        out_specs=out_specs,
        check_vma=False,
    )
```
